32 devices in a mesh: dp: 8 (over z, y), tensor: 4 (over x, core).
Axes of the slice: x: 2, y: 2, z: 4, core: 2. Of those that a mesh axis runs over, the one named last changes fastest.
Arguments:
- layer_input: bfloat16 [196, 64, 768], P('tensor', 'dp'), may hold values from -6 to 6
- image_counts: int32 [8], P('dp'), may hold values from 4 to 8
- expand: bfloat16 [196, 384], P(None, 'tensor'), may hold values from -0.4375 to 0.4375
- uplift: bfloat16 [384], P('tensor'), may hold values from -3 to 3
- contract: bfloat16 [384, 196], P('tensor'), may hold values from -0.3125 to 0.3125
- offset: bfloat16 [196], P('tensor'), may hold values from -3 to 3
- scaling: bfloat16 [768], replicated, may hold values from 0.099609375 to 1.8984375
- centering: bfloat16 [768], replicated, may hold values from -3 to 3
- rescaling: bfloat16 [768], replicated, may hold values from 0.099609375 to 1.8984375
- recentering: bfloat16 [768], replicated, may hold values from -3 to 3
- broaden: bfloat16 [768, 3072], replicated, may hold values from -0.21875 to 0.21875
- raising: bfloat16 [3072], replicated, may hold values from -3 to 3
- narrow: bfloat16 [3072, 768], replicated, may hold values from -0.109375 to 0.109375
- lowering: bfloat16 [768], replicated, may hold values from -3 to 3
- cotangent: bfloat16 [196, 64, 768], P('tensor', 'dp'), may hold values from -6 to 6
Outputs:
- layer_output: bfloat16 [196, 64, 768], P('tensor', 'dp')
- input_grad: bfloat16 [196, 64, 768], P('tensor', 'dp')
- expand_grad: float32 [196, 384], P(None, 'tensor')
- uplift_grad: float32 [384], P('tensor')
- contract_grad: float32 [384, 196], P('tensor')
- offset_grad: float32 [196], P('tensor')
- scaling_grad: float32 [768], replicated
- centering_grad: float32 [768], replicated
- rescaling_grad: float32 [768], replicated
- recentering_grad: float32 [768], replicated
- broaden_grad: float32 [768, 3072], P(None, ('dp', 'tensor'))
- raising_grad: float32 [3072], P(('dp', 'tensor'))
- narrow_grad: float32 [3072, 768], P(('dp', 'tensor'))
- lowering_grad: float32 [768], replicated
The draws below stay inside these ranges and needn't reach their ends.
Inputs may be any that keep to these rules, and one draw needn't show every extreme that they name: `image_counts`: slots of a dp index at or above its count hold padding images.
All inputs are finite; a program needn't handle non-finite values.
Results may differ from the reference program's by a relative error of at most 0.007.
Values may be sent and summed in bfloat16 or wider, within the bound.
A program may use at most 128 MiB of HBM per device.

```python
import jax
import jax.numpy as jnp
from jax import lax

D = 768
S = 196
DS = 384
DC = 3072
IMG_DEV = 8
B = 64
N_DP = 8


def place_ends(values, rng, low, top_value):
    place = [jax.random.randint(jax.random.fold_in(rng, axis), (), 0, length) for axis, length in enumerate(values.shape)]
    longest = values.shape.index(max(values.shape))
    neighbour = place[:longest] + [(place[longest] + 1) % values.shape[longest]] + place[longest + 1:]
    return values.at[tuple(place)].set(low).at[tuple(neighbour)].set(top_value)


def block_scale(key, shape, shards, low, largest):
    gain, own = 1.0, jax.random.fold_in(key, 6)
    for axis_at, shards_of in shards:
        steps = jnp.exp(jax.random.uniform(jax.random.fold_in(own, axis_at), (shards_of,), jnp.float32, low / len(shards), largest / len(shards)))
        gain = gain * jnp.repeat(steps, shape[axis_at] // shards_of).reshape([-1 if axis == axis_at else 1 for axis in range(len(shape))])
    return gain


def normal_values(key, extent, width, most, pieces=(), kind=jnp.bfloat16):
    factor_of = block_scale(key, extent, pieces, -0.22, 0.18) if pieces else 1.0
    entries = jax.random.normal(key, extent, jnp.float32) * width * factor_of
    return jnp.minimum(jnp.maximum(entries, -most), most).astype(kind)


def setup_inputs(seed: int = 0) -> dict:
    key_of = jax.random.split(jax.random.key(seed), 16)
    layer_input = normal_values(key_of[0], (S, B, D), 1.0, 6.0, ((0, 4), (1, 8)))
    image_counts = place_ends(jax.random.randint(key_of[1], (N_DP,), IMG_DEV // 2, IMG_DEV + 1), jax.random.fold_in(key_of[1], 1), IMG_DEV // 2, IMG_DEV).astype(jnp.int32)
    expand = normal_values(key_of[2], (S, DS), S ** -0.5, 0.4375, ((1, 4),))
    uplift = normal_values(key_of[3], (DS,), 0.5, 3.0, ((0, 4),))
    contract = normal_values(key_of[4], (DS, S), DS ** -0.5, 0.3125, ((0, 4),))
    offset = normal_values(key_of[5], (S,), 0.5, 3.0, ((0, 4),))
    scaling = jnp.clip(1.0 + 0.18 * jax.random.normal(key_of[6], (D,), jnp.float32), 0.099609375, 1.8984375).astype(jnp.bfloat16)
    centering = normal_values(key_of[7], (D,), 0.5, 3.0)
    rescaling = jnp.clip(1.0 + 0.18 * jax.random.normal(key_of[8], (D,), jnp.float32), 0.099609375, 1.8984375).astype(jnp.bfloat16)
    recentering = normal_values(key_of[9], (D,), 0.5, 3.0)
    broaden = normal_values(key_of[10], (D, DC), D ** -0.5, 0.21875)
    raising = normal_values(key_of[11], (DC,), 0.5, 3.0)
    narrow = normal_values(key_of[12], (DC, D), DC ** -0.5, 0.109375)
    lowering = normal_values(key_of[13], (D,), 0.5, 3.0)
    cotangent = normal_values(key_of[14], (S, B, D), 1.0, 6.0, ((0, 4), (1, 8)))
    return {"layer_input": layer_input, "image_counts": image_counts, "expand": expand, "uplift": uplift, "contract": contract, "offset": offset, "scaling": scaling, "centering": centering, "rescaling": rescaling, "recentering": recentering, "broaden": broaden, "raising": raising, "narrow": narrow, "lowering": lowering, "cotangent": cotangent}


@jax.custom_vjp
def low(v):
    return lax.optimization_barrier(v.astype(jnp.bfloat16)).astype(jnp.float32)

@jax.custom_vjp
def low_back(v):
    return v

def low_keep(v):
    return (low(v), None)

def low_pass(kept, grad):
    return (grad,)

def back_keep(v):
    return (v, None)

def back_low(kept, grad):
    return (low(grad),)
low.defvjp(low_keep, low_pass)
low_back.defvjp(back_keep, back_low)

def layer_norm(values, scale_vec, shift_vec):
    centre = values - lax.optimization_barrier(jnp.mean(values, axis=-1, keepdims=True))
    spread = lax.optimization_barrier(jnp.mean(centre * centre, axis=-1, keepdims=True))
    return centre * lax.rsqrt(spread + 1e-06) * scale_vec + shift_vec

def forward(block_in, params, image_mask):
    expand, uplift, contract, offset, scaling, centering, rescaling, recentering, broaden, raising, narrow, lowering = params
    highest = lax.Precision.HIGHEST
    images = block_in.shape[1]
    normed = low(layer_norm(block_in, scaling, centering)).reshape(S, images * D)
    token_pre = low_back(jnp.dot(expand.T, normed, precision=highest) + uplift[:, None])
    token_act = low(jax.nn.gelu(token_pre))
    token_out = low_back(jnp.dot(contract.T, token_act, precision=highest) + offset[:, None])
    mixed_rows = (block_in + token_out.reshape(S, images, D)).reshape(S * images, D)
    normed_rows = low(layer_norm(mixed_rows, rescaling, recentering))
    channel_pre = low_back(jnp.dot(normed_rows, broaden, precision=highest) + raising)
    channel_act = low(jax.nn.gelu(channel_pre))
    channel_out = low_back(jnp.dot(channel_act, narrow, precision=highest) + lowering)
    return (mixed_rows + channel_out).reshape(S, images, D) * image_mask[None, :, None]

def reference(layer_input, image_counts, expand, uplift, contract, offset, scaling, centering, rescaling, recentering, broaden, raising, narrow, lowering, cotangent):
    params = tuple((weight.astype(jnp.float32) for weight in (expand, uplift, contract, offset, scaling, centering, rescaling, recentering, broaden, raising, narrow, lowering)))
    blocks_in = layer_input.astype(jnp.float32).reshape(S, N_DP, IMG_DEV, D).transpose(1, 0, 2, 3)
    blocks_ct = cotangent.astype(jnp.float32).reshape(S, N_DP, IMG_DEV, D).transpose(1, 0, 2, 3)

    def one_block(totals, block_items):
        block_in, block_ct, image_count = block_items
        image_mask = (jnp.arange(IMG_DEV, dtype=jnp.int32) < image_count).astype(jnp.float32)

        def apply(values_in, params_in):
            return forward(values_in, params_in, image_mask)
        result, backward = jax.vjp(apply, block_in, params)
        grad_in, grad_params = backward(block_ct)
        totals = tuple((first + second for first, second in zip(totals, grad_params)))
        return (totals, (result.astype(jnp.bfloat16), grad_in.astype(jnp.bfloat16)))
    zero_grads = tuple((jnp.zeros_like(weight) for weight in params))
    totals, (outputs_all, grads_all) = lax.scan(one_block, zero_grads, (blocks_in, blocks_ct, image_counts))
    layer_output = outputs_all.transpose(1, 0, 2, 3).reshape(S, N_DP * IMG_DEV, D)
    input_grad = grads_all.transpose(1, 0, 2, 3).reshape(S, N_DP * IMG_DEV, D)
    return (layer_output, input_grad, totals[0], totals[1], totals[2], totals[3], totals[4], totals[5], totals[6], totals[7], totals[8], totals[9], totals[10], totals[11])
```

```python
import functools

import jax
import jax.numpy as jnp
from jax import lax
from jax.experimental import pallas as pl
from jax.experimental.pallas import tpu as pltpu
from jax.sharding import PartitionSpec as P

MESH = pl.DeviceIdType.MESH
F32 = jnp.float32
BF16 = jnp.bfloat16
EPS = 1e-6


def dot(a, b, ca, cb):
    return lax.dot_general(a, b, (((ca,), (cb,)), ((), ())), preferred_element_type=F32)


def dot_exact(a, b, ca, cb):
    return lax.dot_general(
        a, b, (((ca,), (cb,)), ((), ())), precision=lax.Precision.HIGHEST, preferred_element_type=F32
    )


def gelu_parts(v):
    c = 0.7978845608028654
    v2 = v * v
    t = jnp.tanh(c * v * (1.0 + 0.044715 * v2))
    half = 0.5 + 0.5 * t
    act = v * half
    slope = half + (0.5 * c) * v * (1.0 - t * t) * (1.0 + (3.0 * 0.044715) * v2)
    return act, slope


def norm_stats(v):
    mu = jnp.mean(v, axis=-1, keepdims=True)
    cen = v - mu
    rs = lax.rsqrt(jnp.mean(cen * cen, axis=-1, keepdims=True) + EPS)
    return cen * rs, rs


def norm_back(grad, xhat, rs, gain):
    g = grad * gain
    return rs * (g - jnp.mean(g, axis=-1, keepdims=True) - xhat * jnp.mean(g * xhat, axis=-1, keepdims=True))


class Sizes:
    pass


def kernel(
    z,
    cnt, x, ct_hbm, ex, co, prm, w1_hbm, w2_hbm,
    lo, ig, eg, up, cg, vec, bg, ng,
    ct, w1, w2, xs, sb, rb, et, cc, nb16, tp, ta, mixed, nr, ol, yacc, gacc, mgrad,
    gs, r1, rx0, ry0, rz0, ry1, rz1, rx1, so, ro, so2, ro2,
    vv, vr, ec, ecr, ecs, ecx,
    lsem, a_s, a_r, w_s, w_r, c_s, c_r, x0s, x0r, y0s, y0r, z0s, z0r, y1s, y1r, z1s, z1r, x1s, x1r,
    o_s, o_r, v_s, v_r, e_s, e_r,
):
    D, PT, PP, R, HB, HC, T, NDP = z.D, z.PT, z.PP, z.R, z.HB, z.HC, z.T, z.NDP
    NZ = NDP // 2
    DSL, DS = z.DSL, z.DSL * T
    half_r = R // 2
    dp = lax.axis_index("dp")
    te = lax.axis_index("tensor")
    di = lax.rem(dp, NDP)
    mc = lax.rem(te, 2)
    mx = te // 2
    my = lax.rem(di, 2)
    mz = di // 2

    def tpeer(o):
        if o == 1:
            return te + 1 - 2 * mc
        if o == 2:
            return lax.rem(te + 2, 4)
        return 3 - te

    core_dev = (dp, tpeer(1))
    x_dev = (dp, tpeer(2))
    y_dev = (dp + 1 - 2 * my, te)

    def z_dev(o):
        return (dp - di + lax.rem(di + 2 * o, NDP), te)

    def rc(src, dst, ss, rs, dev):
        return pltpu.make_async_remote_copy(
            src_ref=src, dst_ref=dst, send_sem=ss, recv_sem=rs, device_id=dev, device_id_type=MESH
        )

    lc_ct = pltpu.make_async_copy(ct_hbm, ct, lsem.at[0])
    lc_w1 = pltpu.make_async_copy(w1_hbm, w1, lsem.at[1])
    lc_w2 = pltpu.make_async_copy(w2_hbm, w2, lsem.at[2])
    lc_ct.start()

    peers = [(dp, tpeer(o)) for o in (1, 2, 3)] + [y_dev] + [z_dev(o) for o in range(1, NZ)]
    bar = pltpu.get_barrier_semaphore()
    for dev in peers:
        pl.semaphore_signal(bar, inc=1, device_id=dev, device_id_type=MESH)

    def spread(src, k):
        for c in range(D // 128):
            lanes = slice(c * 128, c * 128 + 128)
            xs[c * PP * 8 : c * PP * 8 + PT * 8, :] = src[:, :, lanes].astype(F32).reshape(PT * 8, 128)
            for j in range(T):
                for b in range(2):
                    piece = xs[pl.ds(c * PP * 8 + 2 * j + b, PP, stride=8), :]
                    sb[k, j, b, :, lanes] = piece.astype(BF16)

    def a2a(k, o, b):
        j = tpeer(o)
        return rc(sb.at[k, j, b], rb.at[k, te, b], a_s.at[k, o - 1, b], a_r.at[k, o - 1, b], (dp, j))

    for c in range(D // 128):
        xs[c * PP * 8 + PT * 8 : (c + 1) * PP * 8, :] = jnp.zeros((PP * 8 - PT * 8, 128), F32)
    spread(x, 0)
    pl.semaphore_wait(bar, len(peers))
    for b in range(2):
        for o in (2, 3, 1):
            a2a(0, o, b).start()
    lc_w1.start()
    lc_w2.start()
    for b in range(2):
        rb[0, te, b] = sb[0, te, b]

    row = lax.broadcasted_iota(jnp.int32, (PT * T, PP * T), 0)
    col = lax.broadcasted_iota(jnp.int32, (PT * T, PP * T), 1)
    pick = jnp.zeros((PT * T, PP * T), F32)
    for t in range(T):
        inside = (col >= PP * t) & (col < PP * t + PT) & (row - PT * t == col - PP * t)
        pick = pick + jnp.where(inside, 1.0, 0.0)
    pick16 = pick.astype(BF16)
    col1 = lax.broadcasted_iota(jnp.int32, (1, PP * T), 1)
    pad_one = jnp.where(col1 == PT, 1.0, 0.0)
    uplift_col = dot_exact(prm[6:7, 0:DSL], pad_one, 0, 0)
    ew = dot(ex[...], pick16, 0, 0) + uplift_col
    cw = dot(co[...], pick16, 1, 0)
    et[te, 0] = ew.astype(BF16)
    et[te, 1] = cw.astype(BF16)
    mine = (col1 >= PP * te) & (col1 < PP * te + PT)
    off_row = jnp.where(mine, prm[5:6, 0 : PP * T], 0.0)
    cc[te] = jnp.broadcast_to(off_row, (8, PP * T))

    def wcopies(o):
        dev = (dp, tpeer(o))
        return (
            rc(et.at[te], et.at[te], w_s.at[0, o - 1], w_r.at[0, o - 1], dev),
            rc(cc.at[te], cc.at[te], w_s.at[1, o - 1], w_r.at[1, o - 1], dev),
        )

    def wrecv(o):
        j = tpeer(o)
        return (
            rc(et.at[j], et.at[j], w_s.at[0, o - 1], w_r.at[0, o - 1], (dp, j)),
            rc(cc.at[j], cc.at[j], w_s.at[1, o - 1], w_r.at[1, o - 1], (dp, j)),
        )

    for o in (2, 3, 1):
        for c in wcopies(o):
            c.start()

    lc_ct.wait()
    spread(ct, 1)
    for b in range(2):
        for o in (2, 3, 1):
            a2a(1, o, b).start()
    for b in range(2):
        rb[1, te, b] = sb[1, te, b]

    def a2a_wait(k, o, b):
        j = tpeer(o)
        rc(sb.at[k, j, b], rb.at[k, j, b], a_s.at[k, o - 1, b], a_r.at[k, o - 1, b], (dp, j)).wait_recv()

    for o in (1, 2, 3):
        for c in wrecv(o):
            c.wait_recv()

    e_t = et[:, 0].reshape(DS, PP * T)
    c_t = et[:, 1].reshape(DS, PP * T)
    zero_pad = lax.broadcasted_iota(jnp.int32, (DS, PP * T), 1) == PT
    e_clean = jnp.where(zero_pad, 0.0, e_t.astype(F32)).astype(BF16)
    off_full = (cc[0] + cc[1]) + (cc[2] + cc[3])
    first8 = lax.broadcasted_iota(jnp.int32, (8, PP * T), 0) == 0
    off_row8 = jnp.where(first8, off_full, 0.0).astype(BF16)
    scaling, centering = prm[0:1, :], prm[1:2, :]
    rescaling, recentering = prm[2:3, :], prm[3:4, :]
    lowering = prm[4:5, :]
    rows_b = lax.broadcasted_iota(jnp.int32, (half_r, 1), 0)
    ones_row = rows_b == PT
    ones8 = jnp.where(lax.broadcasted_iota(jnp.int32, (8, D), 0) == 0, 1.0, 0.0).astype(BF16)

    def image_rows(k, b):
        return jnp.concatenate([rb[k, t, b].astype(F32) for t in range(T)], axis=0)

    for b in range(2):
        for o in (1, 2, 3):
            a2a_wait(0, o, b)
        sl = slice(b * half_r, (b + 1) * half_r)
        xb = image_rows(0, b)
        xhat, _ = norm_stats(xb)
        n = jnp.where(ones_row, 1.0, xhat * scaling + centering).astype(BF16)
        nb16[sl, :] = n
        pre = dot(e_t, n, 1, 0)
        tp[b] = pre
        act, _ = gelu_parts(pre)
        ta[b, 0:DS, :] = act.astype(BF16)
        ta[b, DS : DS + 8, :] = ones8
        tok = dot(c_t, ta[b, 0:DS, :], 0, 0) + dot(off_row8, ones8, 0, 0)
        mx_b = xb + tok
        mixed[sl, :] = mx_b
        xh2, _ = norm_stats(mx_b)
        nr[sl, :] = (xh2 * rescaling + recentering).astype(BF16)

    low_sum = jnp.zeros((1, D), F32)
    for b in range(2):
        for o in (1, 2, 3):
            a2a_wait(1, o, b)
        sl = slice(b * half_r, (b + 1) * half_r)
        keep = jnp.where(2 * te + b < cnt[0], 1.0, 0.0)
        og = image_rows(1, b) * keep
        ol[sl, :] = og.astype(BF16)
        low_sum = low_sum + jnp.sum(og, axis=0, keepdims=True)
    vv[...] = jnp.zeros(vv.shape, F32)
    vv[4:5, :] = low_sum
    yacc[...] = jnp.zeros(yacc.shape, F32)
    gacc[...] = jnp.zeros(gacc.shape, F32)
    lc_w1.wait()
    lc_w2.wait()

    def add_into(dst, src):
        dst[...] = (dst[...].astype(F32) + src[...].astype(F32)).astype(BF16)

    def core_copy(i):
        return rc(gs.at[i, 1 - mc], r1.at[i], c_s.at[i], c_r.at[i], core_dev)

    def x0_copy(i):
        return rc(gs.at[i, mc, 0, 1 - mx], rx0.at[i], x0s.at[i], x0r.at[i], x_dev)

    def y1_copy(i):
        return rc(gs.at[i, mc, 1], ry1.at[i], y1s.at[i], y1r.at[i], y_dev)

    def after_core(i):
        core_copy(i).wait_recv()
        for g in range(2):
            for xx in range(2):
                add_into(gs.at[i, mc, g, xx], r1.at[i, g, xx])
        x0_copy(i).start()

    def block(i, carry):
        other = jnp.where(i < NZ, 1, 0)
        zz = lax.rem(mz + 1 + lax.rem(i, NZ), NZ)
        yy = lax.rem(my + other, 2)
        d = zz * 2 + yy
        cols = pl.ds(pl.multiple_of(d * HB, HB), HB)
        w1d = w1[:, cols]
        w2d = w2[cols, :]
        pre = dot(nr[...], w1d, 1, 0) + prm[pl.ds(8 + d, 1), 0:HB]
        act, slope = gelu_parts(pre)
        act16 = act.astype(BF16)
        back = dot(ol[...], w2d, 1, 1)
        low32 = slope * back
        low16 = low32.astype(BF16)
        yacc[...] += dot(act16, w2d, 1, 0)
        gacc[...] += dot(low16, w1d, 1, 1)
        gn = dot(act16, ol[...], 0, 0)
        gb = dot(low16, nr[...], 0, 0)
        for t in range(T):
            gs[i, t % 2, 0, t // 2] = gn[t * HC : (t + 1) * HC, :].astype(BF16)
            gs[i, t % 2, 1, t // 2] = gb[t * HC : (t + 1) * HC, :].astype(BF16)
        vv[pl.ds(8 + d, 1), 0:HB] = jnp.sum(low16.astype(F32), axis=0, keepdims=True)
        core_copy(i).start()

        @pl.when(i > 0)
        def _():
            after_core(i - 1)

            @pl.when(i - 1 < NZ)
            def _():
                y1_copy(i - 1).start()

        return carry

    lax.fori_loop(0, NDP, block, 0)
    after_core(NDP - 1)

    def ocopy(k, o):
        src, dst = (so, ro) if k == 0 else (so2, ro2)
        j = tpeer(o)
        return rc(src.at[j], dst.at[te], o_s.at[k, o - 1], o_r.at[k, o - 1], (dp, j))

    def ocopy_in(k, o):
        src, dst = (so, ro) if k == 0 else (so2, ro2)
        j = tpeer(o)
        return rc(src.at[j], dst.at[j], o_s.at[k, o - 1], o_r.at[k, o - 1], (dp, j))

    for b in range(2):
        keep = jnp.where(2 * te + b < cnt[0], 1.0, 0.0)
        for t in range(T):
            r0 = b * half_r + t * PP
            sl = slice(r0, r0 + PP)
            so[t, b] = ((mixed[sl, :] + yacc[sl, :] + lowering) * keep).astype(BF16)
    for o in (2, 3, 1):
        ocopy(0, o).start()
    ro[te] = so[te]

    resc_sum = jnp.zeros((1, D), F32)
    rece_sum = jnp.zeros((1, D), F32)
    for b in range(2):
        sl = slice(b * half_r, (b + 1) * half_r)
        xh2, rs2 = norm_stats(mixed[sl, :])
        gr = gacc[sl, :]
        resc_sum = resc_sum + jnp.sum(gr * xh2, axis=0, keepdims=True)
        rece_sum = rece_sum + jnp.sum(gr, axis=0, keepdims=True)
        mgrad[sl, :] = ol[sl, :].astype(F32) + norm_back(gr, xh2, rs2, rescaling)
    vv[2:3, :] = resc_sum
    vv[3:4, :] = rece_sum

    eg_sum = jnp.zeros((DS, PP * T), F32)
    cg_sum = jnp.zeros((DS + 8, PP * T), F32)
    scal_sum = jnp.zeros((1, D), F32)
    cent_sum = jnp.zeros((1, D), F32)
    for b in range(2):
        sl = slice(b * half_r, (b + 1) * half_r)
        ml = mgrad[sl, :].astype(BF16)
        _, slope = gelu_parts(tp[b])
        tg = (slope * dot(c_t, ml, 1, 0)).astype(BF16)
        cg_sum = cg_sum + dot(ta[b], ml, 1, 1)
        eg_sum = eg_sum + dot(tg, nb16[sl, :], 1, 1)
        nback = dot(e_clean, tg, 0, 0)
        xhat, rs1 = norm_stats(image_rows(0, b))
        scal_sum = scal_sum + jnp.sum(nback * xhat, axis=0, keepdims=True)
        cent_sum = cent_sum + jnp.sum(nback, axis=0, keepdims=True)
        grad = (mgrad[sl, :] + norm_back(nback, xhat, rs1, scaling)).astype(BF16)
        for t in range(T):
            so2[t, b] = grad[t * PP : (t + 1) * PP, :]
    for o in (2, 3, 1):
        ocopy(1, o).start()
    ro2[te] = so2[te]
    vv[0:1, :] = scal_sum
    vv[1:2, :] = cent_sum
    vv[5:6, 0 : PP * T] = cg_sum[DS : DS + 1, :]
    for t in range(T):
        ec[t % 2, t // 2, 0] = eg_sum[t * DSL : (t + 1) * DSL, :]
        ec[t % 2, t // 2, 1] = cg_sum[t * DSL : (t + 1) * DSL, :]

    def e_core():
        return rc(ec.at[1 - mc], ecr, e_s.at[0], e_r.at[0], core_dev)

    def v_copy(s, dev):
        return rc(vv, vr.at[s], v_s.at[s], v_r.at[s], dev)

    e_core().start()
    v_copy(0, core_dev).start()
    e_core().wait_recv()
    ecs[0] = (ec[mc, 1 - mx] + ecr[1 - mx]).astype(BF16)
    own_ec = ec[mc, mx] + ecr[mx]

    def e_x():
        return rc(ecs.at[0], ecx.at[0], e_s.at[1], e_r.at[1], x_dev)

    e_x().start()
    v_copy(0, core_dev).wait()
    vv[...] = vv[...] + vr[0]
    v_copy(1, x_dev).start()

    for q in range(NZ):
        y1_copy(q).wait_recv()
        for xx in range(2):
            add_into(gs.at[NZ + q, mc, 1, xx], ry1.at[q, xx])
        if q < NZ - 1:
            rc(gs.at[NZ + q, mc, 1], rz1.at[q], z1s.at[q], z1r.at[q], z_dev(q + 1)).start()

    e_x().wait_recv()
    own_ec = own_ec + ecx[0].astype(F32)
    ecs[1] = own_ec.astype(BF16)

    def e_y():
        return rc(ecs.at[1], ecx.at[1], e_s.at[2], e_r.at[2], y_dev)

    e_y().start()
    v_copy(1, x_dev).wait()
    vv[...] = vv[...] + vr[1]
    v_copy(2, y_dev).start()

    def y0_copy(q):
        return rc(gs.at[q, mc, 0, mx], ry0.at[q], y0s.at[q], y0r.at[q], y_dev)

    for i in range(NDP):
        x0_copy(i).wait_recv()
        add_into(gs.at[i, mc, 0, mx], rx0.at[i])
        if i < NZ:
            y0_copy(i).start()

    e_y().wait_recv()
    own_ec = own_ec + ecx[1].astype(F32)
    ecs[2] = own_ec.astype(BF16)

    def e_z(o):
        return rc(ecs.at[2], ecx.at[1 + o], e_s.at[2 + o], e_r.at[2 + o], z_dev(o))

    def v_z(o):
        return rc(vv, vr.at[2 + o], v_s.at[2 + o], v_r.at[2 + o], z_dev(o))

    for o in range(1, NZ):
        e_z(o).start()
    v_copy(2, y_dev).wait()
    vv[...] = vv[...] + vr[2]
    for o in range(1, NZ):
        v_z(o).start()

    for q in range(NZ):
        y0_copy(q).wait_recv()
        add_into(gs.at[NZ + q, mc, 0, mx], ry0.at[q])
        if q < NZ - 1:
            rc(gs.at[NZ + q, mc, 0, mx], rz0.at[q], z0s.at[q], z0r.at[q], z_dev(q + 1)).start()

    for q in range(NZ - 1):
        rc(gs.at[NZ + q, mc, 1], rz1.at[q], z1s.at[q], z1r.at[q], z_dev(q + 1)).wait_recv()

    def z_total(xx):
        tot = gs[NDP - 1, mc, 1, xx].astype(F32)
        for q in range(NZ - 1):
            tot = tot + rz1[q, xx].astype(F32)
        return tot

    r1[0, 0, 0] = z_total(1 - mx).astype(BF16)
    own_b = z_total(mx)
    x1 = rc(r1.at[0, 0, 0], rx1, x1s, x1r, x_dev)
    x1.start()

    def collect(k, dst):
        src = ro if k == 0 else ro2
        for o in (1, 2, 3):
            ocopy_in(k, o).wait_recv()
        for c in range(D // 128):
            lanes = slice(c * 128, c * 128 + 128)
            for j in range(T):
                for b in range(2):
                    xs[pl.ds(c * PP * 8 + 2 * j + b, PP, stride=8), :] = src[j, b, :, lanes].astype(F32)
            dst[:, :, lanes] = xs[c * PP * 8 : c * PP * 8 + PT * 8, :].reshape(PT, 8, 128).astype(BF16)

    collect(0, lo)
    collect(1, ig)

    for o in range(1, NZ):
        e_z(o).wait_recv()
        v_z(o).wait_recv()
    tot_ec = own_ec
    tot_v = vv[...]
    for o in range(1, NZ):
        tot_ec = tot_ec + ecx[1 + o].astype(F32)
        tot_v = tot_v + vr[2 + o]
    vec[...] = tot_v
    eg[...] = dot_exact(pick, tot_ec[0], 1, 1)
    cg[...] = dot_exact(tot_ec[1], pick, 1, 1)
    up[...] = dot_exact(jnp.broadcast_to(pad_one, (8, PP * T)), tot_ec[0], 1, 1)

    for q in range(NZ - 1):
        rc(gs.at[NZ + q, mc, 0, mx], rz0.at[q], z0s.at[q], z0r.at[q], z_dev(q + 1)).wait_recv()
    tot = gs[NDP - 1, mc, 0, mx].astype(F32)
    for q in range(NZ - 1):
        tot = tot + rz0[q].astype(F32)
    ng[...] = tot
    x1.wait_recv()
    bg[...] = jnp.transpose(own_b + rx1[...].astype(F32))

    for k in range(2):
        for o in (1, 2, 3):
            for b in range(2):
                a2a(k, o, b).wait_send()
            ocopy(k, o).wait_send()
    for o in (1, 2, 3):
        for c in wcopies(o):
            c.wait_send()
    for i in range(NDP):
        core_copy(i).wait_send()
        x0_copy(i).wait_send()
    for q in range(NZ):
        y1_copy(q).wait_send()
        y0_copy(q).wait_send()
    for q in range(NZ - 1):
        rc(gs.at[NZ + q, mc, 1], rz1.at[q], z1s.at[q], z1r.at[q], z_dev(q + 1)).wait_send()
        rc(gs.at[NZ + q, mc, 0, mx], rz0.at[q], z0s.at[q], z0r.at[q], z_dev(q + 1)).wait_send()
    x1.wait_send()
    e_core().wait_send()
    e_x().wait_send()
    e_y().wait_send()
    for o in range(1, NZ):
        e_z(o).wait_send()
        v_z(o).wait_send()


def local(
    layer_input, image_counts, expand, uplift, contract, offset, scaling, centering,
    rescaling, recentering, broaden, raising, narrow, lowering, cotangent, *, mesh,
):
    z = Sizes()
    z.PT, images, z.D = layer_input.shape
    z.T, z.NDP = mesh.shape["tensor"], 8
    outer = mesh.shape["dp"] // z.NDP
    z.PP = -(-(z.PT + 1) // 8) * 8
    z.R = 2 * z.T * z.PP
    hidden = broaden.shape[1]
    if outer > 1:
        split = (outer, z.NDP, z.T, hidden // (outer * z.NDP * z.T))
        broaden = broaden.reshape(-1, *split).transpose(0, 2, 3, 1, 4).reshape(-1, hidden)
        raising = raising.reshape(split).transpose(1, 2, 0, 3).reshape(hidden)
        narrow = narrow.reshape(*split, -1).transpose(1, 2, 0, 3, 4).reshape(hidden, -1)
    z.HB = hidden // z.NDP
    z.HC = z.HB // z.T
    z.DSL = expand.shape[1]
    D, T, NDP, PP, PT, R, HB, HC, DSL = z.D, z.T, z.NDP, z.PP, z.PT, z.R, z.HB, z.HC, z.DSL
    DS, NZ = DSL * T, NDP // 2

    def line(v):
        return jnp.pad(v.astype(F32), (0, D - v.shape[0]))[None]

    off_line = jnp.tile(jnp.pad(offset.astype(F32), (0, PP - PT)), T)
    prm = jnp.concatenate(
        [line(v) for v in (scaling, centering, rescaling, recentering, lowering, off_line, uplift)]
        + [jnp.zeros((1, D), F32), jnp.pad(raising.astype(F32).reshape(NDP, HB), ((0, 0), (0, D - HB)))],
        axis=0,
    )
    vm = pl.BlockSpec(memory_space=pltpu.VMEM)
    anys = pl.BlockSpec(memory_space=pl.ANY)
    dma = pltpu.SemaphoreType.DMA
    V = pltpu.VMEM
    scratch = [
        V((PT, 8, D), BF16), V(broaden.shape, BF16), V(narrow.shape, BF16), V((D // 128 * PP * 8, 128), F32),
        V((2, T, 2, PP, D), BF16), V((2, T, 2, PP, D), BF16), V((T, 2, DSL, PP * T), BF16), V((T, 8, PP * T), F32),
        V((R, D), BF16), V((2, DS, D), F32), V((2, DS + 8, D), BF16), V((R, D), F32), V((R, D), BF16), V((R, D), BF16),
        V((R, D), F32), V((R, D), F32), V((R, D), F32),
        V((NDP, 2, 2, 2, HC, D), BF16), V((NDP, 2, 2, HC, D), BF16), V((NDP, HC, D), BF16), V((NZ, HC, D), BF16),
        V((NZ - 1, HC, D), BF16), V((NZ, 2, HC, D), BF16), V((NZ - 1, 2, HC, D), BF16), V((HC, D), BF16),
        V((T, 2, PP, D), BF16), V((T, 2, PP, D), BF16), V((T, 2, PP, D), BF16), V((T, 2, PP, D), BF16),
        V((16, D), F32), V((2 + NZ, 16, D), F32), V((2, 2, 2, DSL, PP * T), F32), V((2, 2, DSL, PP * T), F32),
        V((3, 2, DSL, PP * T), BF16), V((1 + NZ, 2, DSL, PP * T), BF16),
        dma((3,)), dma((2, 3, 2)), dma((2, 3, 2)), dma((2, 3)), dma((2, 3)), dma((NDP,)), dma((NDP,)),
        dma((NDP,)), dma((NDP,)), dma((NZ,)), dma((NZ,)), dma((NZ - 1,)), dma((NZ - 1,)),
        dma((NZ,)), dma((NZ,)), dma((NZ - 1,)), dma((NZ - 1,)), dma(()), dma(()),
        dma((2, 3)), dma((2, 3)), dma((2 + NZ,)), dma((2 + NZ,)), dma((2 + NZ,)), dma((2 + NZ,)),
    ]
    S = jax.ShapeDtypeStruct
    outs = pl.pallas_call(
        functools.partial(kernel, z),
        out_shape=(
            S((PT, images, D), BF16), S((PT, images, D), BF16), S((PT * T, DSL), F32), S((8, DSL), F32),
            S((DSL, PT * T), F32), S((16, D), F32), S((D, HC), F32), S((HC, D), F32),
        ),
        in_specs=[pl.BlockSpec(memory_space=pltpu.SMEM), vm, anys, vm, vm, vm, anys, anys],
        out_specs=(vm,) * 8,
        scratch_shapes=scratch,
        compiler_params=pltpu.CompilerParams(
            collective_id=0, has_side_effects=True, vmem_limit_bytes=62 * 1024 * 1024
        ),
    )(image_counts, layer_input, cotangent, expand, contract, prm, broaden, narrow)
    lo, ig, eg, up, cg, vec, bg, ng = outs
    te, dp = lax.axis_index("tensor"), lax.rem(lax.axis_index("dp"), NDP)
    off = lax.dynamic_slice(vec, (5, te * PP), (1, PT))[0]
    rg = lax.dynamic_slice(vec, (8 + dp, te * HC), (1, HC))[0]
    if outer > 1:
        same = [[o * NDP + i for o in range(outer)] for i in range(NDP)]
        eg, up, cg, off, vec = lax.psum((eg, up, cg, off, vec), "dp", axis_index_groups=same)
        bg = lax.psum_scatter(bg.T, "dp", scatter_dimension=0, axis_index_groups=same, tiled=True).T
        ng = lax.psum_scatter(ng, "dp", scatter_dimension=0, axis_index_groups=same, tiled=True)
        rg = lax.psum_scatter(rg, "dp", scatter_dimension=0, axis_index_groups=same, tiled=True)
    return lo, ig, eg, up[0], cg, off, vec[0], vec[1], vec[2], vec[3], bg, rg, ng, vec[4]


def solution(mesh):
    rows = P("tensor", "dp", None)
    both = ("dp", "tensor")
    in_specs = (
        rows, P("dp"), P(None, "tensor"), P("tensor"), P("tensor", None), P("tensor"),
        P(), P(), P(), P(), P(), P(), P(), P(), rows,
    )
    out_specs = (
        rows, rows, P(None, "tensor"), P("tensor"), P("tensor", None), P("tensor"),
        P(), P(), P(), P(), P(None, both), P(both), P(both, None), P(),
    )
    return jax.shard_map(
        functools.partial(local, mesh=mesh), mesh=mesh, in_specs=in_specs, out_specs=out_specs, check_vma=False
    )
```

```python
import functools

import jax
import jax.numpy as jnp
from jax import lax
from jax.experimental import pallas as pl
from jax.experimental.pallas import tpu as pltpu
from jax.sharding import PartitionSpec as P

MESH = pl.DeviceIdType.MESH
F32 = jnp.float32
BF16 = jnp.bfloat16
EPS = 1e-6
LANES = 128


def dot(a, b, ca, cb):
    return lax.dot_general(a, b, (((ca,), (cb,)), ((), ())), preferred_element_type=F32)


def dot_exact(a, b, ca, cb):
    return lax.dot_general(
        a, b, (((ca,), (cb,)), ((), ())), precision=lax.Precision.HIGHEST, preferred_element_type=F32
    )


def gelu_parts(v):
    c = 0.7978845608028654
    v2 = v * v
    t = jnp.tanh(c * v * (1.0 + 0.044715 * v2))
    half = 0.5 + 0.5 * t
    act = v * half
    slope = half + (0.5 * c) * v * (1.0 - t * t) * (1.0 + (3.0 * 0.044715) * v2)
    return act, slope


def norm_stats(v):
    cen = v - jnp.mean(v, axis=-1, keepdims=True)
    rs = lax.rsqrt(jnp.mean(cen * cen, axis=-1, keepdims=True) + EPS)
    return cen * rs, rs


def norm_back(grad, xhat, rs, gain):
    g = grad * gain
    return rs * (g - jnp.mean(g, axis=-1, keepdims=True) - xhat * jnp.mean(g * xhat, axis=-1, keepdims=True))


def pick_matrix(T, PT, PP):
    row = lax.broadcasted_iota(jnp.int32, (PT * T, PP * T), 0)
    col = lax.broadcasted_iota(jnp.int32, (PT * T, PP * T), 1)
    pick = jnp.zeros((PT * T, PP * T), F32)
    for t in range(T):
        inside = (col >= PP * t) & (col < PP * t + PT) & (row - PT * t == col - PP * t)
        pick = pick + jnp.where(inside, 1.0, 0.0)
    return pick


class Sizes:
    pass


ORDER = ((1, 1, 1), (1, 0, 1), (0, 1, 1), (0, 0, 1), (1, 1, 0), (1, 0, 0), (0, 1, 0), (0, 0, 0))


def layer_kernel(
    z,
    cnt, x, ct_hbm, ex, co, uplift, offset, scal, cent, resc, rece, lowr, rais, w1_hbm, w2_hbm,
    ro, ro2, fin, ecf, vec,
    ct, w1, w2, xs, sb, rb, et, cc, nb16, tp, ta, mixed, nr, ol, yacc, gacc, mgrad, bias, so, so2,
    gs, r1, rxp, ryp, rap, rbp, ryq, raq, rxq, rbq, rar, ryr, rxr, rbr,
    vv, vr, ec, ecr, es, er, tg16,
    lsem, a_s, a_r, w_s, w_r, c_s, c_r, xp_s, xp_r, yp_s, yp_r, ap_s, ap_r, bp_s, bp_r,
    yq_s, yq_r, aq_s, aq_r, xq_s, xq_r, bq_s, bq_r, ar_s, ar_r, yr_s, yr_r, xr_s, xr_r, br_s, br_r,
    o_s, o_r, v_s, v_r, e_s, e_r,
):
    D, PT, PP, R, HB, HC, T, NDP = z.D, z.PT, z.PP, z.R, z.HB, z.HC, z.T, z.NDP
    DSL, DS = z.DSL, z.DSL * T
    PL = PP * T
    half_r = R // 2
    dp = lax.axis_index("dp")
    te = lax.axis_index("tensor")
    di = lax.rem(dp, NDP)
    mc = lax.rem(te, 2)
    mx = te // 2
    my = lax.rem(di, 2)
    mz = di // 2

    def tpeer(o):
        if o == 1:
            return te + 1 - 2 * mc
        if o == 2:
            return lax.rem(te + 2, 4)
        return 3 - te

    core_dev = (dp, tpeer(1))
    x_dev = (dp, tpeer(2))
    y_dev = (dp + 1 - 2 * my, te)

    a_dev = (dp + 2 - 4 * lax.rem(mz, 2), te)
    b_dev = (dp - di + lax.rem(di + 4, NDP), te)
    ma, mb = lax.rem(mz, 2), mz // 2

    def rc(src, dst, ss, rs, dev):
        return pltpu.make_async_remote_copy(
            src_ref=src, dst_ref=dst, send_sem=ss, recv_sem=rs, device_id=dev, device_id_type=MESH
        )

    sent = []

    def send(copy):
        copy.start()
        sent.append(copy)

    lc_ct = pltpu.make_async_copy(ct_hbm, ct, lsem.at[0])
    lc_w1 = pltpu.make_async_copy(w1_hbm, w1, lsem.at[1])
    lc_w2 = pltpu.make_async_copy(w2_hbm, w2, lsem.at[2])
    lc_ct.start()

    peers = [(dp, tpeer(o)) for o in (1, 2, 3)] + [y_dev, a_dev, b_dev]
    bar = pltpu.get_barrier_semaphore()
    for dev in peers:
        pl.semaphore_signal(bar, inc=1, device_id=dev, device_id_type=MESH)

    def spread(src, k):
        for c in range(D // LANES):
            lanes = slice(c * LANES, (c + 1) * LANES)
            xs[c * PP * 8 : c * PP * 8 + PT * 8, :] = src[:, :, lanes].astype(F32).reshape(PT * 8, LANES)
            for j in range(T):
                for b in range(2):
                    sb[k, j, b, :, lanes] = xs[pl.ds(c * PP * 8 + 2 * j + b, PP, stride=8), :].astype(BF16)

    def a2a(k, o, b):
        j = tpeer(o)
        return rc(sb.at[k, j, b], rb.at[k, te, b], a_s.at[k, o - 1, b], a_r.at[k, o - 1, b], (dp, j))

    def a2a_in(k, o, b):
        j = tpeer(o)
        return rc(sb.at[k, j, b], rb.at[k, j, b], a_s.at[k, o - 1, b], a_r.at[k, o - 1, b], (dp, j))

    for c in range(D // LANES):
        xs[c * PP * 8 + PT * 8 : (c + 1) * PP * 8, :] = jnp.zeros((PP * 8 - PT * 8, LANES), F32)
    spread(x, 0)

    pick = pick_matrix(T, PT, PP)
    pick16 = pick.astype(BF16)
    col1 = lax.broadcasted_iota(jnp.int32, (1, PL), 1)
    pad_one = jnp.where(col1 == PT, 1.0, 0.0)
    uplift_col = dot_exact(uplift[...].astype(F32).reshape(1, DSL), pad_one, 0, 0)
    et[te, 0] = (dot(ex[...], pick16, 1, 0) + uplift_col).astype(BF16)
    et[te, 1] = dot(co[...], pick16, 1, 0).astype(BF16)
    off_line = offset[...].astype(F32).reshape(1, PT)
    own_cols = (lax.broadcasted_iota(jnp.int32, (PT, PL), 1) - PP * te) == lax.broadcasted_iota(
        jnp.int32, (PT, PL), 0
    )
    off_row = dot(off_line.astype(BF16), jnp.where(own_cols, 1.0, 0.0).astype(BF16), 1, 0)
    cc[te] = jnp.broadcast_to(off_row, (8, PL))

    pl.semaphore_wait(bar, len(peers))

    def wcopies(t, slot, dev):
        return [
            rc(et.at[t], et.at[t], w_s.at[0, slot], w_r.at[0, slot], dev),
            rc(cc.at[t], cc.at[t], w_s.at[1, slot], w_r.at[1, slot], dev),
        ]

    for o in (2, 3, 1):
        send(a2a(0, o, 0))
    for c in wcopies(te, 1, x_dev) + wcopies(te, 0, core_dev):
        send(c)
    for o in (2, 3, 1):
        send(a2a(0, o, 1))
    for b in range(2):
        rb[0, te, b] = sb[0, te, b]

    lc_ct.wait()
    lc_w1.start()
    lc_w2.start()
    spread(ct, 1)
    for b in range(2):
        for o in (2, 3, 1):
            send(a2a(1, o, b))
    for b in range(2):
        rb[1, te, b] = sb[1, te, b]

    for c in wcopies(tpeer(2), 1, x_dev):
        c.wait_recv()
    for c in wcopies(tpeer(2), 2, core_dev):
        send(c)
    bias_line = rais[...].astype(F32).reshape(1, HB * NDP)
    for d in range(NDP):
        bias[d : d + 1, :] = bias_line[:, d * HB : (d + 1) * HB]
    scaling, centering = scal[...].astype(F32).reshape(1, D), cent[...].astype(F32).reshape(1, D)
    rescaling, recentering = resc[...].astype(F32).reshape(1, D), rece[...].astype(F32).reshape(1, D)
    lowering = lowr[...].astype(F32).reshape(1, D)
    for c in wcopies(tpeer(1), 0, core_dev) + wcopies(tpeer(3), 2, core_dev):
        c.wait_recv()

    e_t = et[:, 0].reshape(DS, PL)
    c_t = et[:, 1].reshape(DS, PL)
    zero_pad = lax.broadcasted_iota(jnp.int32, (DS, PL), 1) == PT
    e_clean = jnp.where(zero_pad, 0.0, e_t.astype(F32)).astype(BF16)
    off_full = (cc[0] + cc[1]) + (cc[2] + cc[3])
    first8 = lax.broadcasted_iota(jnp.int32, (8, PL), 0) == 0
    off_row8 = jnp.where(first8, off_full, 0.0).astype(BF16)
    ones_row = lax.broadcasted_iota(jnp.int32, (half_r, 1), 0) == PT
    ones8 = jnp.where(lax.broadcasted_iota(jnp.int32, (8, D), 0) == 0, 1.0, 0.0).astype(BF16)

    def image_rows(k, b):
        return jnp.concatenate([rb[k, t, b].astype(F32) for t in range(T)], axis=0)

    for b in range(2):
        for o in (1, 2, 3):
            a2a_in(0, o, b).wait_recv()
        sl = slice(b * half_r, (b + 1) * half_r)
        xb = image_rows(0, b)
        xhat, _ = norm_stats(xb)
        n = jnp.where(ones_row, 1.0, xhat * scaling + centering).astype(BF16)
        nb16[sl, :] = n
        pre = dot(e_t, n, 1, 0)
        tp[b] = pre
        act, _ = gelu_parts(pre)
        ta[b, 0:DS, :] = act.astype(BF16)
        ta[b, DS : DS + 8, :] = ones8
        mx_b = xb + dot(c_t, ta[b, 0:DS, :], 0, 0) + dot(off_row8, ones8, 0, 0)
        mixed[sl, :] = mx_b
        xh2, _ = norm_stats(mx_b)
        nr[sl, :] = (xh2 * rescaling + recentering).astype(BF16)

    low_sum = jnp.zeros((1, D), F32)
    for b in range(2):
        for o in (1, 2, 3):
            a2a_in(1, o, b).wait_recv()
        sl = slice(b * half_r, (b + 1) * half_r)
        keep = jnp.where(2 * te + b < cnt[0], 1.0, 0.0)
        og = image_rows(1, b) * keep
        ol[sl, :] = og.astype(BF16)
        low_sum = low_sum + jnp.sum(og, axis=0, keepdims=True)
    vv[0] = jnp.zeros(vv.shape[1:], F32)
    vv[0, 4:5, :] = low_sum
    yacc[...] = jnp.zeros(yacc.shape, F32)
    gacc[...] = jnp.zeros(gacc.shape, F32)
    lc_w1.wait()
    lc_w2.wait()

    PR, QR, RR = pl.ds(0, z.P), pl.ds(z.P, z.Q), pl.ds(z.P + z.Q, HC - z.P - z.Q)
    pos = {o: i for i, o in enumerate(ORDER)}

    def add_into(dst, src):
        dst[...] = (dst[...].astype(F32) + src[...].astype(F32)).astype(BF16)

    def core_copy(i):
        return rc(gs.at[i, 1 - mc], r1.at[i], c_s.at[i], c_r.at[i], core_dev)

    def xp_copy(i):
        return rc(gs.at[i, mc, 1 - mx, :, PR], rxp.at[i], xp_s.at[i], xp_r.at[i], x_dev)

    def yq_copy(i):
        return rc(gs.at[i, mc, :, :, QR], ryq.at[i], yq_s.at[i], yq_r.at[i], y_dev)

    def ar_copy(i):
        return rc(gs.at[i, mc, :, :, RR], rar.at[i], ar_s.at[i], ar_r.at[i], a_dev)

    def after_core(i):
        core_copy(i).wait_recv()
        for xx in range(2):
            for g in range(2):
                add_into(gs.at[i, mc, xx, g], r1.at[i, xx, g])
        xp_copy(i).start()

    def among(i, bit):
        hit = jnp.int32(0)
        for k, o in enumerate(ORDER):
            if o[bit]:
                hit = hit + jnp.where(i == k, 1, 0)
        return hit

    def flip(m, bit):
        return m + bit - 2 * m * bit

    def begin(copy):
        copy.start()

    def add_rows(i, rows, src, both):
        for g in range(2):
            if both:
                for xx in range(2):
                    add_into(gs.at[i, mc, xx, g, rows], src.at[xx, g])
            else:
                add_into(gs.at[i, mc, mx, g, rows], src.at[g])

    def own(i, rows):
        return gs.at[i, mc, mx, :, rows]

    def oth(i, rows):
        return gs.at[i, mc, 1 - mx, :, rows]

    def yp_copy(da, db):
        k = 2 * da + db
        return rc(own(pos[1, da, db], PR), ryp.at[k], yp_s.at[k], yp_r.at[k], y_dev)

    def ap_copy(db):
        return rc(own(pos[0, 1, db], PR), rap.at[db], ap_s.at[db], ap_r.at[db], a_dev)

    bp_copy = rc(own(pos[0, 0, 1], PR), rbp, bp_s, bp_r, b_dev)

    def take_xp(o, send=send):
        xp_copy(pos[o]).wait_recv()
        add_rows(pos[o], PR, rxp.at[pos[o]], False)
        if o[0]:
            send(yp_copy(o[1], o[2]))

    def take_yp(da, db):
        yp_copy(da, db).wait_recv()
        add_rows(pos[0, da, db], PR, ryp.at[2 * da + db], False)
        if da:
            send(ap_copy(db))

    def take_ap(db):
        ap_copy(db).wait_recv()
        add_rows(pos[0, 0, db], PR, rap.at[db], False)
        if db:
            send(bp_copy)

    def aq_copy(db):
        return rc(gs.at[pos[0, 1, db], mc, :, :, QR], raq.at[db], aq_s.at[db], aq_r.at[db], a_dev)

    def xq_copy(db):
        return rc(oth(pos[0, 0, db], QR), rxq.at[db], xq_s.at[db], xq_r.at[db], x_dev)

    bq_copy = rc(own(pos[0, 0, 1], QR), rbq, bq_s, bq_r, b_dev)

    def take_yq(da, db, send=send):
        yq_copy(pos[1, da, db]).wait_recv()
        add_rows(pos[0, da, db], QR, ryq.at[pos[1, da, db]], True)
        if da:
            send(aq_copy(db))

    def take_aq(db):
        aq_copy(db).wait_recv()
        add_rows(pos[0, 0, db], QR, raq.at[db], True)
        send(xq_copy(db))

    def take_xq(db):
        xq_copy(db).wait_recv()
        add_rows(pos[0, 0, db], QR, rxq.at[db], False)
        if db:
            send(bq_copy)

    def yr_copy(db):
        return rc(gs.at[pos[1, 0, db], mc, :, :, RR], ryr.at[db], yr_s.at[db], yr_r.at[db], y_dev)

    def xr_copy(db):
        return rc(oth(pos[0, 0, db], RR), rxr.at[db], xr_s.at[db], xr_r.at[db], x_dev)

    br_copy = rc(own(pos[0, 0, 1], RR), rbr, br_s, br_r, b_dev)

    def take_ar(dy, db, send=send):
        ar_copy(pos[dy, 1, db]).wait_recv()
        add_rows(pos[dy, 0, db], RR, rar.at[pos[dy, 1, db]], True)
        if dy:
            send(yr_copy(db))

    def take_yr(db):
        yr_copy(db).wait_recv()
        add_rows(pos[0, 0, db], RR, ryr.at[db], True)
        send(xr_copy(db))

    def take_xr(db):
        xr_copy(db).wait_recv()
        add_rows(pos[0, 0, db], RR, rxr.at[db], False)
        if db:
            send(br_copy)

    def block(i, carry):
        d = flip(mb, among(i, 2)) * 4 + flip(ma, among(i, 1)) * 2 + flip(my, among(i, 0))
        cols = pl.ds(pl.multiple_of(d * HB, HB), HB)
        w1d = w1[:, cols]
        w2d = w2[cols, :]
        pre = dot(nr[...], w1d, 1, 0) + bias[pl.ds(d, 1), :]
        act, slope = gelu_parts(pre)
        act16 = act.astype(BF16)
        low16 = (slope * dot(ol[...], w2d, 1, 1)).astype(BF16)
        gn = dot(act16, ol[...], 0, 0)
        gb = dot(low16, nr[...], 0, 0)
        for t in range(T):
            rows = slice(t * HC, (t + 1) * HC)
            gs[i, t % 2, t // 2, 0] = gn[rows, :].astype(BF16)
            gs[i, t % 2, t // 2, 1] = gb[rows, :].astype(BF16)
        core_copy(i).start()
        yacc[...] += dot(act16, w2d, 1, 0)
        gacc[...] += dot(low16, w1d, 1, 1)
        vv[0, pl.ds(8 + d, 1), 0:HB] = jnp.sum(low16.astype(F32), axis=0, keepdims=True)

        @pl.when(i > 0)
        def _():
            after_core(i - 1)

            @pl.when(among(i - 1, 0) == 1)
            def _():
                yq_copy(i - 1).start()

            @pl.when(among(i - 1, 1) == 1)
            def _():
                ar_copy(i - 1).start()

        @pl.when(i == 5)
        def _():
            take_yq(1, 1, begin)
            take_ar(1, 1, begin)
            take_xp((1, 1, 1), begin)
            take_xp((1, 0, 1), begin)

        @pl.when(i == 6)
        def _():
            take_yq(0, 1, begin)
            take_ar(0, 1, begin)
            take_xp((0, 1, 1), begin)
            take_xp((0, 0, 1), begin)

        return carry

    lax.fori_loop(0, NDP, block, 0)
    after_core(NDP - 1)
    sent.extend([aq_copy(1), yr_copy(1), yp_copy(1, 1), yp_copy(0, 1)])
    sent.extend([core_copy(i) for i in range(NDP)] + [xp_copy(i) for i in range(NDP)])
    sent.extend([yq_copy(i) for i, o in enumerate(ORDER) if o[0]] + [ar_copy(i) for i, o in enumerate(ORDER) if o[1]])

    def ocopy(k, o, b):
        src, dst = (so, ro) if k == 0 else (so2, ro2)
        j = tpeer(o)
        return rc(src.at[j, b], dst.at[te, b], o_s.at[k, o - 1, b], o_r.at[k, o - 1, b], (dp, j))

    def ocopy_in(k, o, b):
        src, dst = (so, ro) if k == 0 else (so2, ro2)
        j = tpeer(o)
        return rc(src.at[j, b], dst.at[j, b], o_s.at[k, o - 1, b], o_r.at[k, o - 1, b], (dp, j))

    lc_o = [pltpu.make_async_copy(s.at[te], r.at[te], lsem.at[3 + k]) for k, (s, r) in enumerate(((so, ro), (so2, ro2)))]

    def out_image(b):
        keep = jnp.where(2 * te + b < cnt[0], 1.0, 0.0)
        for t in range(T):
            r0 = b * half_r + t * PP
            sl = slice(r0, r0 + PP)
            so[t, b] = ((mixed[sl, :] + yacc[sl, :] + lowering) * keep).astype(BF16)
        for o in (2, 3, 1):
            send(ocopy(0, o, b))

    take_aq(1)
    take_yr(1)
    out_image(0)

    resc_sum = jnp.zeros((1, D), F32)
    rece_sum = jnp.zeros((1, D), F32)
    for b in range(2):
        sl = slice(b * half_r, (b + 1) * half_r)
        xh2, rs2 = norm_stats(mixed[sl, :])
        gr = gacc[sl, :]
        resc_sum = resc_sum + jnp.sum(gr * xh2, axis=0, keepdims=True)
        rece_sum = rece_sum + jnp.sum(gr, axis=0, keepdims=True)
        mgrad[sl, :] = ol[sl, :].astype(F32) + norm_back(gr, xh2, rs2, rescaling)
    vv[0, 2:3, :] = resc_sum
    vv[0, 3:4, :] = rece_sum

    take_yq(1, 0)
    take_ar(1, 0)
    take_xp((1, 1, 0))
    take_xp((1, 0, 0))

    eg_sum = jnp.zeros((DS, PL), F32)
    cg_sum = jnp.zeros((DS + 8, PL), F32)
    for b in range(2):
        sl = slice(b * half_r, (b + 1) * half_r)
        ml = mgrad[sl, :].astype(BF16)
        _, slope = gelu_parts(tp[b])
        tg = (slope * dot(c_t, ml, 1, 0)).astype(BF16)
        tg16[b] = tg
        cg_sum = cg_sum + dot(ta[b], ml, 1, 1)
        eg_sum = eg_sum + dot(tg, nb16[sl, :], 1, 1)
    vv[0, 5:6, 0:PL] = cg_sum[DS : DS + 1, :]
    for t in range(T):
        ec[t % 2, t // 2, 0] = eg_sum[t * DSL : (t + 1) * DSL, :]
        ec[t % 2, t // 2, 1] = cg_sum[t * DSL : (t + 1) * DSL, :]

    def v_copy(s, dev):
        return rc(vv.at[s], vr.at[s], v_s.at[s], v_r.at[s], dev)

    def e_copy(s, dev):
        return rc(es.at[s], er.at[s], e_s.at[s + 1], e_r.at[s + 1], dev)

    def v_next(s, dev, nxt):
        v_copy(s, dev).wait_recv()
        vv[s + 1] = vv[s] + vr[s]
        if nxt is not None:
            send(v_copy(s + 1, nxt))

    def e_next(s, dev, nxt):
        e_copy(s, dev).wait_recv()
        if s == 0:
            tot = ec[mc, mx] + ecr[mx] + er[s].astype(F32)
        else:
            tot = es[s].astype(F32) + er[s].astype(F32)
        if nxt is None:
            ecf[...] = tot
        else:
            es[s + 1] = tot.astype(BF16)
            send(e_copy(s + 1, nxt))

    e_core = rc(ec.at[1 - mc], ecr, e_s.at[0], e_r.at[0], core_dev)
    send(e_core)

    def first_back(b):
        nback = dot(e_clean, tg16[b], 0, 0)
        xhat, rs1 = norm_stats(image_rows(0, b))
        sl = slice(b * half_r, (b + 1) * half_r)
        grad = (mgrad[sl, :] + norm_back(nback, xhat, rs1, scaling)).astype(BF16)
        for t in range(T):
            so2[t, b] = grad[t * PP : (t + 1) * PP, :]
        return jnp.sum(nback * xhat, axis=0, keepdims=True), jnp.sum(nback, axis=0, keepdims=True)

    scal0, cent0 = first_back(0)
    e_core.wait_recv()
    es[0] = (ec[mc, 1 - mx] + ecr[1 - mx]).astype(BF16)
    send(e_copy(0, x_dev))
    scal1, cent1 = first_back(1)
    vv[0, 0:1, :] = scal0 + scal1
    vv[0, 1:2, :] = cent0 + cent1
    send(v_copy(0, core_dev))
    take_yp(1, 1)
    take_yp(0, 1)
    take_yq(0, 0)
    take_ar(0, 0)
    take_xp((0, 1, 0))
    take_xp((0, 0, 0))
    v_next(0, core_dev, x_dev)
    take_xq(1)
    take_xr(1)
    out_image(1)
    lc_o[0].start()
    take_aq(0)
    take_yr(0)
    for b in range(2):
        for o in (2, 3, 1):
            send(ocopy(1, o, b))
    lc_o[1].start()
    e_next(0, x_dev, y_dev)
    v_next(1, x_dev, y_dev)
    take_ap(1)
    take_yp(1, 0)
    take_yp(0, 0)
    e_next(1, y_dev, a_dev)
    v_next(2, y_dev, a_dev)
    take_xq(0)
    take_xr(0)
    take_ap(0)
    e_next(2, a_dev, b_dev)
    v_next(3, a_dev, b_dev)

    def last(copy, rows, buf):
        copy.wait_recv()
        for g in range(2):
            fin[g, rows, :] = gs[NDP - 1, mc, mx, g, rows, :].astype(F32) + buf[g].astype(F32)

    last(bq_copy, QR, rbq)
    last(br_copy, RR, rbr)
    last(bp_copy, PR, rbp)
    e_next(3, b_dev, None)
    v_next(4, b_dev, None)
    vec[...] = vv[5]
    for k in range(2):
        for o in (1, 2, 3):
            for b in range(2):
                ocopy_in(k, o, b).wait_recv()
        lc_o[k].wait()

    for c in sent:
        c.wait_send()


def finish_kernel(
    z, ro_h, ro2_h, fin_h, ecf_h, vec_h, lo, ig, eg, up, cg, off, v0, v1, v2, v3, bg, rg, ng, v4,
    xs, ro, ro2, ecf, vec, sem,
):
    D, PT, PP, HB, HC, T, NDP, DSL = z.D, z.PT, z.PP, z.HB, z.HC, z.T, z.NDP, z.DSL
    te = lax.axis_index("tensor")
    di = lax.rem(lax.axis_index("dp"), NDP)
    pairs = ((ro_h, ro), (ro2_h, ro2), (ecf_h, ecf), (vec_h, vec), (fin_h.at[0], ng), (fin_h.at[1], bg))
    loads = [pltpu.make_async_copy(src, dst, sem.at[k]) for k, (src, dst) in enumerate(pairs)]
    for c in loads:
        c.start()
    for k, (src, dst) in enumerate(((ro, lo), (ro2, ig))):
        loads[k].wait()
        for c in range(D // LANES):
            lanes = slice(c * LANES, (c + 1) * LANES)
            for j in range(T):
                for b in range(2):
                    xs[pl.ds(c * PP * 8 + 2 * j + b, PP, stride=8), :] = src[j, b, :, lanes].astype(F32)
            dst[:, :, lanes] = xs[c * PP * 8 : c * PP * 8 + PT * 8, :].reshape(PT, 8, LANES).astype(BF16)
    for c in loads[2:]:
        c.wait()
    pick = pick_matrix(T, PT, PP)
    eg[...] = dot_exact(ecf[0], pick, 1, 1)
    cg[...] = dot_exact(ecf[1], pick, 1, 1)
    row8 = lax.broadcasted_iota(jnp.int32, (8, PP * T), 1)
    up[...] = dot_exact(jnp.where(row8 == PT, 1.0, 0.0), ecf[0], 1, 1)[0:1, :].reshape(DSL)
    for ref, r in ((v0, 0), (v1, 1), (v2, 2), (v3, 3), (v4, 4)):
        ref[...] = vec[r : r + 1, :].reshape(D)
    off_row = vec[5:6, :]
    rg_row = vec[pl.ds(8 + di, 1), :]
    off_own = jnp.zeros((1, PT), F32)
    rg_own = jnp.zeros((1, HC), F32)
    for t in range(T):
        off_own = off_own + jnp.where(te == t, off_row[:, t * PP : t * PP + PT], 0.0)
        rg_own = rg_own + jnp.where(te == t, rg_row[:, t * HC : (t + 1) * HC], 0.0)
    off[...] = off_own.reshape(PT)
    rg[...] = rg_own.reshape(HC)


def local(
    layer_input, image_counts, expand, uplift, contract, offset, scaling, centering,
    rescaling, recentering, broaden, raising, narrow, lowering, cotangent, *, mesh,
):
    z = Sizes()
    z.PT, images, z.D = layer_input.shape
    z.T, z.NDP = mesh.shape["tensor"], 8
    outer = mesh.shape["dp"] // z.NDP
    z.PP = -(-(z.PT + 1) // 8) * 8
    z.R = 2 * z.T * z.PP
    hidden = broaden.shape[1]
    if outer > 1:
        split = (outer, z.NDP, z.T, hidden // (outer * z.NDP * z.T))
        broaden = broaden.reshape(-1, *split).transpose(0, 2, 3, 1, 4).reshape(-1, hidden)
        raising = raising.reshape(split).transpose(1, 2, 0, 3).reshape(hidden)
        narrow = narrow.reshape(*split, -1).transpose(1, 2, 0, 3, 4).reshape(hidden, -1)
    z.HB = hidden // z.NDP
    z.HC = z.HB // z.T
    z.DSL = expand.shape[1]
    D, T, NDP, PP, PT, R, HB, HC, DSL = z.D, z.T, z.NDP, z.PP, z.PT, z.R, z.HB, z.HC, z.DSL
    DS, PL = DSL * T, PP * T

    vm = pl.BlockSpec(memory_space=pltpu.VMEM)
    anys = pl.BlockSpec(memory_space=pl.ANY)
    dma = pltpu.SemaphoreType.DMA
    V = pltpu.VMEM
    S = jax.ShapeDtypeStruct
    z.P, z.Q = HC // 3, HC // 3
    P_, Q_, R_ = z.P, z.Q, HC - z.P - z.Q
    sems = []
    for shape in (
        (2, 3, 2), (2, 3), (NDP,), (NDP,), (4,), (2,), (), (NDP,), (2,), (2,), (), (NDP,), (2,), (2,), (),
        (2, 3, 2), (5,), (5,),
    ):
        sems += [dma(shape), dma(shape)]
    scratch = [
        V((PT, 8, D), BF16), V(broaden.shape, BF16), V(narrow.shape, BF16), V((D // LANES * PP * 8, LANES), F32),
        V((2, T, 2, PP, D), BF16), V((2, T, 2, PP, D), BF16), V((T, 2, DSL, PL), BF16), V((T, 8, PL), F32),
        V((R, D), BF16), V((2, DS, D), F32), V((2, DS + 8, D), BF16), V((R, D), F32), V((R, D), BF16), V((R, D), BF16),
        V((R, D), F32), V((R, D), F32), V((R, D), F32), V((NDP, HB), F32), V((T, 2, PP, D), BF16), V((T, 2, PP, D), BF16),
        V((NDP, 2, 2, 2, HC, D), BF16), V((NDP, 2, 2, HC, D), BF16),
        V((NDP, 2, P_, D), BF16), V((4, 2, P_, D), BF16), V((2, 2, P_, D), BF16), V((2, P_, D), BF16),
        V((NDP, 2, 2, Q_, D), BF16), V((2, 2, 2, Q_, D), BF16), V((2, 2, Q_, D), BF16), V((2, Q_, D), BF16),
        V((NDP, 2, 2, R_, D), BF16), V((2, 2, 2, R_, D), BF16), V((2, 2, R_, D), BF16), V((2, R_, D), BF16),
        V((6, 16, D), F32), V((5, 16, D), F32), V((2, 2, 2, DSL, PL), F32), V((2, 2, DSL, PL), F32),
        V((4, 2, DSL, PL), BF16), V((4, 2, DSL, PL), BF16), V((2, DS, D), BF16),
        dma((5,)),
    ] + sems
    mid = pl.pallas_call(
        functools.partial(layer_kernel, z),
        out_shape=(
            S((T, 2, PP, D), BF16), S((T, 2, PP, D), BF16), S((2, HC, D), F32), S((2, DSL, PL), F32), S((16, D), F32),
        ),
        in_specs=[pl.BlockSpec(memory_space=pltpu.SMEM), vm, anys] + [vm] * 10 + [anys, anys],
        out_specs=(anys, anys, vm, vm, vm),
        scratch_shapes=scratch,
        compiler_params=pltpu.CompilerParams(
            collective_id=0, has_side_effects=True, vmem_limit_bytes=60 * 1024 * 1024
        ),
    )(
        image_counts, layer_input, cotangent, expand.T, contract, uplift, offset, scaling, centering,
        rescaling, recentering, lowering, raising, broaden, narrow,
    )
    res = pl.pallas_call(
        functools.partial(finish_kernel, z),
        out_shape=(
            S((PT, images, D), BF16), S((PT, images, D), BF16), S((DSL, PT * T), F32), S((DSL,), F32),
            S((DSL, PT * T), F32), S((PT,), F32), S((D,), F32), S((D,), F32), S((D,), F32), S((D,), F32),
            S((HC, D), F32), S((HC,), F32), S((HC, D), F32), S((D,), F32),
        ),
        in_specs=[anys] * 5,
        out_specs=(vm,) * 14,
        scratch_shapes=[
            V((D // LANES * PP * 8, LANES), F32), V((T, 2, PP, D), BF16), V((T, 2, PP, D), BF16), V((2, DSL, PL), F32),
            V((16, D), F32), dma((6,)),
        ],
        compiler_params=pltpu.CompilerParams(vmem_limit_bytes=60 * 1024 * 1024),
    )(*mid)
    lo, ig, eg, up, cg, off, v0, v1, v2, v3, bg, rg, ng, v4 = res
    if outer > 1:
        same = [[o * NDP + i for o in range(outer)] for i in range(NDP)]
        eg, up, cg, off, v0, v1, v2, v3, v4 = lax.psum(
            (eg, up, cg, off, v0, v1, v2, v3, v4), "dp", axis_index_groups=same
        )
        bg, ng, rg = (
            lax.psum_scatter(v, "dp", scatter_dimension=0, axis_index_groups=same, tiled=True) for v in (bg, ng, rg)
        )
    return lo, ig, eg.T, up, cg, off, v0, v1, v2, v3, bg.T, rg, ng, v4


def solution(mesh):
    rows = P("tensor", "dp", None)
    both = ("dp", "tensor")
    in_specs = (
        rows, P("dp"), P(None, "tensor"), P("tensor"), P("tensor", None), P("tensor"),
        P(), P(), P(), P(), P(), P(), P(), P(), rows,
    )
    out_specs = (
        rows, rows, P(None, "tensor"), P("tensor"), P("tensor", None), P("tensor"),
        P(), P(), P(), P(), P(None, both), P(both), P(both, None), P(),
    )
    return jax.shard_map(
        functools.partial(local, mesh=mesh), mesh=mesh, in_specs=in_specs, out_specs=out_specs, check_vma=False
    )
```

```python
import functools

import jax
import jax.numpy as jnp
from jax import lax
from jax.experimental import pallas as pl
from jax.experimental.pallas import tpu as pltpu
from jax.sharding import PartitionSpec as P

MESH = pl.DeviceIdType.MESH
F32 = jnp.float32
BF16 = jnp.bfloat16
EPS = 1e-6
LANES = 128


def dot(a, b, ca, cb):
    return lax.dot_general(a, b, (((ca,), (cb,)), ((), ())), preferred_element_type=F32)


def dot_exact(a, b, ca, cb):
    return lax.dot_general(
        a, b, (((ca,), (cb,)), ((), ())), precision=lax.Precision.HIGHEST, preferred_element_type=F32
    )


def gelu_parts(v):
    c = 0.7978845608028654
    v2 = v * v
    t = jnp.tanh(c * v * (1.0 + 0.044715 * v2))
    half = 0.5 + 0.5 * t
    act = v * half
    slope = half + (0.5 * c) * v * (1.0 - t * t) * (1.0 + (3.0 * 0.044715) * v2)
    return act, slope


def norm_stats(v):
    cen = v - jnp.mean(v, axis=-1, keepdims=True)
    rs = lax.rsqrt(jnp.mean(cen * cen, axis=-1, keepdims=True) + EPS)
    return cen * rs, rs


def norm_back(grad, xhat, rs, gain):
    g = grad * gain
    return rs * (g - jnp.mean(g, axis=-1, keepdims=True) - xhat * jnp.mean(g * xhat, axis=-1, keepdims=True))


def pick_matrix(T, PT, PP):
    row = lax.broadcasted_iota(jnp.int32, (PT * T, PP * T), 0)
    col = lax.broadcasted_iota(jnp.int32, (PT * T, PP * T), 1)
    pick = jnp.zeros((PT * T, PP * T), F32)
    for t in range(T):
        inside = (col >= PP * t) & (col < PP * t + PT) & (row - PT * t == col - PP * t)
        pick = pick + jnp.where(inside, 1.0, 0.0)
    return pick


class Sizes:
    pass


ORDER = ((1, 1, 1), (0, 1, 1), (1, 0, 1), (0, 0, 1), (1, 1, 0), (0, 1, 0), (1, 0, 0), (0, 0, 0))

EARLY = (
    (1, (
        ("yq", 1, 1), ("ar", 1, 1),
    )),
)
LATE = (
    ("yq", 0, 1), ("ar", 0, 1), ("yr", 1), ("ln2",), ("xp", 1, 0, 1), ("tok",), ("xp", 0, 0, 1), ("xp", 1, 1, 1),
    ("xp", 0, 1, 0), ("f", 0), ("xp", 0, 1, 1), ("aq", 1), ("e", 0), ("lo", 0), ("yq", 1, 0), ("f", 1),
    ("xp", 1, 1, 0), ("xp", 0, 0, 0), ("xr", 1), ("xq", 1), ("ar", 0, 0), ("v", 0), ("e", 1), ("v", 1), ("ar", 1, 0),
    ("ig", 0), ("yp", 1, 1), ("e", 2), ("yq", 0, 0), ("aq", 0), ("yp", 0, 1), ("ap", 1), ("yp", 1, 0), ("v", 2),
    ("lo", 1), ("e", 3), ("v", 3), ("yr", 0), ("xp", 1, 0, 0), ("ig", 1), ("xq", 0), ("v", 4), ("yp", 0, 0),
    ("v", 5), ("ap", 0), ("xr", 0), ("e", 4),
)


def layer_kernel(
    z,
    cnt, x, ct_hbm, ex, co, uplift, offset, scal, cent, resc, rece, lowr, rais, w1_hbm, w2_hbm,
    ro, ro2, fin, ecf, vec,
    ct, w1, w2, xs, sb, rb, et, cc, nb16, tp, ta, mixed, nr, ol, yacc, gacc, mgrad, bias, so, so2, ext, act_s, low_s, sums,
    gs, r1, rxp, ryp, rap, rbp, ryq, raq, rxq, rbq, rar, ryr, rxr, rbr,
    vv, vr, ec, ecr, es, er, tg16,
    lsem, a_s, a_r, w_s, w_r, c_s, c_r, xp_s, xp_r, yp_s, yp_r, ap_s, ap_r, bp_s, bp_r,
    yq_s, yq_r, aq_s, aq_r, xq_s, xq_r, bq_s, bq_r, ar_s, ar_r, yr_s, yr_r, xr_s, xr_r, br_s, br_r,
    o_s, o_r, v_s, v_r, e_s, e_r,
):
    D, PT, PP, R, HB, HC, T, NDP = z.D, z.PT, z.PP, z.R, z.HB, z.HC, z.T, z.NDP
    DSL, DS = z.DSL, z.DSL * T
    PL = PP * T
    half_r = R // 2
    dp = lax.axis_index("dp")
    te = lax.axis_index("tensor")
    di = lax.rem(dp, NDP)
    mc = lax.rem(te, 2)
    mx = te // 2
    my = lax.rem(di, 2)
    mz = di // 2

    def tpeer(o):
        if o == 1:
            return te + 1 - 2 * mc
        if o == 2:
            return lax.rem(te + 2, 4)
        return 3 - te

    core_dev = (dp, tpeer(1))
    x_dev = (dp, tpeer(2))
    y_dev = (dp + 1 - 2 * my, te)

    a_dev = (dp + 2 - 4 * lax.rem(mz, 2), te)
    b_dev = (dp - di + lax.rem(di + 4, NDP), te)
    ma, mb = lax.rem(mz, 2), mz // 2

    def rc(src, dst, ss, rs, dev):
        return pltpu.make_async_remote_copy(
            src_ref=src, dst_ref=dst, send_sem=ss, recv_sem=rs, device_id=dev, device_id_type=MESH
        )

    sent = []

    def send(copy):
        copy.start()
        sent.append(copy)

    lc_ct = pltpu.make_async_copy(ct_hbm, ct, lsem.at[0])
    lc_w1 = pltpu.make_async_copy(w1_hbm, w1, lsem.at[1])
    lc_w2 = pltpu.make_async_copy(w2_hbm, w2, lsem.at[2])
    lc_ct.start()

    peers = [(dp, tpeer(o)) for o in (1, 2, 3)] + [y_dev, a_dev, b_dev]
    bar = pltpu.get_barrier_semaphore()
    for dev in peers:
        pl.semaphore_signal(bar, inc=1, device_id=dev, device_id_type=MESH)

    row8 = lax.broadcasted_iota(jnp.int32, (8, LANES), 0)
    PM = PT - PT % 8
    IMG = (slice(0, PM), slice(PP, PP + PM))
    IN = (pl.ds(0, PP), pl.ds(PP, PM))
    OUT = (pl.ds(0, PM), pl.ds(PM, PP))

    def spread(src, k):
        for c in range(D // LANES):
            lanes = slice(c * LANES, (c + 1) * LANES)
            base = c * PT * 8
            xs[base : base + PT * 8, :] = src[:, :, lanes].astype(F32).reshape(PT * 8, LANES)
            tail = xs[base + PM * 8 : base + PT * 8, :]
            for j in range(T):
                for b in range(2):
                    sb[k, j, IMG[b], lanes] = xs[pl.ds(base + 2 * j + b, PM, stride=8), :].astype(BF16)
                two = tail if j == 0 else pltpu.roll(tail, 8 - 2 * j, 0)
                sb[k, j, PM:PP, lanes] = jnp.where(row8 < 2, two, 0.0).astype(BF16)

    def a2a(k, o, b):
        j = tpeer(o)
        return rc(sb.at[k, j, IN[b]], rb.at[k, te, IN[b]], a_s.at[k, o - 1, b], a_r.at[k, o - 1, b], (dp, j))

    def a2a_in(k, o, b):
        j = tpeer(o)
        return rc(sb.at[k, j, IN[b]], rb.at[k, j, IN[b]], a_s.at[k, o - 1, b], a_r.at[k, o - 1, b], (dp, j))

    spread(x, 0)

    pick = pick_matrix(T, PT, PP)
    pick16 = pick.astype(BF16)
    col1 = lax.broadcasted_iota(jnp.int32, (1, PL), 1)
    pad_one = jnp.where(col1 == PT, 1.0, 0.0)
    uplift_col = dot_exact(uplift[...].astype(F32).reshape(1, DSL), pad_one, 0, 0)
    et[te, 0] = (dot(ex[...], pick16, 1, 0) + uplift_col).astype(BF16)
    et[te, 1] = dot(co[...], pick16, 1, 0).astype(BF16)
    off_line = offset[...].astype(F32).reshape(1, PT)
    own_cols = (lax.broadcasted_iota(jnp.int32, (PT, PL), 1) - PP * te) == lax.broadcasted_iota(
        jnp.int32, (PT, PL), 0
    )
    off_row = dot(off_line.astype(BF16), jnp.where(own_cols, 1.0, 0.0).astype(BF16), 1, 0)
    cc[te] = jnp.broadcast_to(off_row, (8, PL))

    pl.semaphore_wait(bar, len(peers))

    tx, t3 = tpeer(2), tpeer(3)

    def wcopy(k, ref, dev):
        return rc(ref, ref, w_s.at[k], w_r.at[k], dev)

    send(wcopy(0, et.at[te, my], x_dev))
    send(wcopy(1, cc.at[te], x_dev))
    for b in range(2):
        for o in (2, 3, 1):
            send(a2a(0, o, b))
    send(wcopy(2, et.at[te], core_dev))
    send(wcopy(3, cc.at[te], core_dev))
    rb[0, te] = sb[0, te]

    lc_ct.wait()
    lc_w1.start()
    lc_w2.start()
    spread(ct, 1)
    for b in range(2):
        for o in (2, 3, 1):
            send(a2a(1, o, b))
    rb[1, te] = sb[1, te]

    wcopy(0, et.at[tx, my], x_dev).wait_recv()
    send(wcopy(4, et.at[tx, my], y_dev))
    wcopy(1, cc.at[tx], x_dev).wait_recv()
    send(wcopy(5, et.at[tx, my], core_dev))
    send(wcopy(6, cc.at[tx], core_dev))
    bias_line = rais[...].astype(F32).reshape(1, HB * NDP)
    for m in range(NDP // 2):
        bias[m : m + 1, :] = bias_line[:, 2 * m * HB : 2 * (m + 1) * HB]
    scaling, centering = scal[...].astype(F32).reshape(1, D), cent[...].astype(F32).reshape(1, D)
    rescaling, recentering = resc[...].astype(F32).reshape(1, D), rece[...].astype(F32).reshape(1, D)
    lowering = lowr[...].astype(F32).reshape(1, D)
    wcopy(4, et.at[tx, 1 - my], y_dev).wait_recv()
    send(wcopy(7, et.at[tx, 1 - my], core_dev))
    tc = tpeer(1)
    for k, ref in ((2, et.at[tc]), (3, cc.at[tc]), (5, et.at[t3, my]), (6, cc.at[t3]), (7, et.at[t3, 1 - my])):
        wcopy(k, ref, core_dev).wait_recv()

    e_t = et[:, 0].reshape(DS, PL)
    c_t = et[:, 1].reshape(DS, PL)
    zero_pad = lax.broadcasted_iota(jnp.int32, (DS, PL), 1) == PT
    e_clean = jnp.where(zero_pad, 0.0, e_t.astype(F32)).astype(BF16)
    off_full = (cc[0] + cc[1]) + (cc[2] + cc[3])
    first8 = lax.broadcasted_iota(jnp.int32, (8, PL), 0) == 0
    off_row8 = jnp.where(first8, off_full, 0.0).astype(BF16)
    ones_row = lax.broadcasted_iota(jnp.int32, (half_r, 1), 0) == PT
    row8d = lax.broadcasted_iota(jnp.int32, (8, D), 0)
    ones8 = jnp.where(row8d == 0, 1.0, 0.0).astype(BF16)

    def image_rows(k, b):
        pieces = []
        for t in range(T):
            tail = rb[k, t, PM:PP, :].astype(F32)
            tail = pltpu.roll(tail, 7, 0) if b else tail
            pieces += [rb[k, t, IMG[b], :].astype(F32), jnp.where(row8d == 0, tail, 0.0)]
        return jnp.concatenate(pieces, axis=0)

    for b in range(2):
        for o in (1, 2, 3):
            a2a_in(0, o, b).wait_recv()
        sl = slice(b * half_r, (b + 1) * half_r)
        xb = image_rows(0, b)
        xhat, _ = norm_stats(xb)
        n = jnp.where(ones_row, 1.0, xhat * scaling + centering).astype(BF16)
        nb16[sl, :] = n
        pre = dot(e_t, n, 1, 0)
        tp[b] = pre
        act, _ = gelu_parts(pre)
        ta[b, 0:DS, :] = act.astype(BF16)
        ta[b, DS : DS + 8, :] = ones8
        mx_b = xb + dot(c_t, ta[b, 0:DS, :], 0, 0) + dot(off_row8, ones8, 0, 0)
        mixed[sl, :] = mx_b
        xh2, _ = norm_stats(mx_b)
        nr[sl, :] = (xh2 * rescaling + recentering).astype(BF16)

    low_sum = jnp.zeros((1, D), F32)
    for b in range(2):
        for o in (1, 2, 3):
            a2a_in(1, o, b).wait_recv()
        sl = slice(b * half_r, (b + 1) * half_r)
        keep = jnp.where(2 * te + b < cnt[0], 1.0, 0.0)
        og = image_rows(1, b) * keep
        ol[sl, :] = og.astype(BF16)
        low_sum = low_sum + jnp.sum(og, axis=0, keepdims=True)
    vv[0] = jnp.zeros(vv.shape[1:], F32)
    vv[0, 4:5, 0:D] = low_sum
    yacc[...] = jnp.zeros(yacc.shape, F32)
    gacc[...] = jnp.zeros(gacc.shape, F32)
    lc_w1.wait()
    lc_w2.wait()

    PR, QR, RR = pl.ds(0, z.P), pl.ds(z.P, z.Q), pl.ds(z.P + z.Q, HC - z.P - z.Q)
    pos = {o: i for i, o in enumerate(ORDER)}

    def add_into(dst, src):
        dst[...] = (dst[...].astype(F32) + src[...].astype(F32)).astype(BF16)

    def flip(m, bit):
        return m + bit - 2 * m * bit

    def piece(o, rows, xx):
        if xx is None:
            return gs.at[pos[o], mc, :, :, rows]
        return gs.at[pos[o], mc, xx, :, rows]

    def core_copy(i):
        return rc(gs.at[i, 1 - mc], r1.at[i], c_s.at[i], c_r.at[i], core_dev)

    def xp_copy(i):
        return rc(gs.at[i, mc, 1 - mx, :, PR], rxp.at[i], xp_s.at[i], xp_r.at[i], x_dev)

    def yq_copy(i):
        k = i // 2
        return rc(gs.at[i, mc, :, :, QR], ryq.at[k], yq_s.at[k], yq_r.at[k], y_dev)

    def ar_copy(i):
        k = i // 4 * 2 + i % 2
        return rc(gs.at[i, mc, :, :, RR], rar.at[k], ar_s.at[k], ar_r.at[k], a_dev)

    def yp_copy(da, db):
        k = 2 * da + db
        return rc(piece((1, da, db), PR, mx), ryp.at[k], yp_s.at[k], yp_r.at[k], y_dev)

    def ap_copy(db):
        return rc(piece((0, 1, db), PR, mx), rap.at[db], ap_s.at[db], ap_r.at[db], a_dev)

    def aq_copy(db):
        return rc(piece((0, 1, db), QR, None), raq.at[db], aq_s.at[db], aq_r.at[db], a_dev)

    def xq_copy(db):
        return rc(piece((0, 0, db), QR, 1 - mx), rxq.at[db], xq_s.at[db], xq_r.at[db], x_dev)

    def yr_copy(db):
        return rc(piece((1, 0, db), RR, None), ryr.at[db], yr_s.at[db], yr_r.at[db], y_dev)

    def xr_copy(db):
        return rc(piece((0, 0, db), RR, 1 - mx), rxr.at[db], xr_s.at[db], xr_r.at[db], x_dev)

    bp_copy = rc(piece((0, 0, 1), PR, mx), rbp, bp_s, bp_r, b_dev)
    bq_copy = rc(piece((0, 0, 1), QR, mx), rbq, bq_s, bq_r, b_dev)
    br_copy = rc(piece((0, 0, 1), RR, mx), rbr, br_s, br_r, b_dev)

    def xp(dy, da, db):
        o = (dy, da, db)
        return xp_copy(pos[o]), o, PR, rxp.at[pos[o]], False, [yp_copy(da, db)] if dy else []

    def yp(da, db):
        return yp_copy(da, db), (0, da, db), PR, ryp.at[2 * da + db], False, [ap_copy(db)] if da else []

    def ap(db):
        return ap_copy(db), (0, 0, db), PR, rap.at[db], False, [bp_copy] if db else []

    def yq(da, db):
        i = pos[1, da, db]
        return yq_copy(i), (0, da, db), QR, ryq.at[i // 2], True, [aq_copy(db)] if da else []

    def aq(db):
        return aq_copy(db), (0, 0, db), QR, raq.at[db], True, [xq_copy(db)]

    def xq(db):
        return xq_copy(db), (0, 0, db), QR, rxq.at[db], False, [bq_copy] if db else []

    def ar(dy, db):
        i = pos[dy, 1, db]
        return ar_copy(i), (dy, 0, db), RR, rar.at[i // 4 * 2 + i % 2], True, [yr_copy(db)] if dy else []

    def yr(db):
        return yr_copy(db), (0, 0, db), RR, ryr.at[db], True, [xr_copy(db)]

    def xr(db):
        return xr_copy(db), (0, 0, db), RR, rxr.at[db], False, [br_copy] if db else []

    steps = dict(xp=xp, yp=yp, ap=ap, yq=yq, aq=aq, xq=xq, ar=ar, yr=yr, xr=xr)

    def take(name, *bits):
        arrival, o, rows, src, both, on = steps[name](*bits)
        arrival.wait_recv()
        for g in range(2):
            if both:
                for xx in range(2):
                    add_into(gs.at[pos[o], mc, xx, g, rows], src.at[xx, g])
            else:
                add_into(gs.at[pos[o], mc, mx, g, rows], src.at[g])
        for c in on:
            c.start()
        return on

    def block(k, carry):
        da, db = 1 - lax.rem(k, 2), 1 - k // 2
        m = flip(mb, db) * 2 + flip(ma, da)
        cols = pl.ds(pl.multiple_of(m * 2 * HB, 2 * HB), 2 * HB)
        pre = dot(nr[...], w1[:, cols], 1, 0) + bias[pl.ds(m, 1), :]
        act, slope = gelu_parts(pre)
        act_s[...] = act.astype(BF16)
        low16 = (slope * dot(ol[...], w2[cols, :], 1, 1)).astype(BF16)
        low_s[...] = low16
        line = jnp.sum(low16.astype(F32), axis=0, keepdims=True)
        for y in range(2):
            vv[0, pl.ds(2 * m + y, 1), D : D + HB] = line[:, y * HB : (y + 1) * HB]
        for h, y in ((0, 1 - my), (1, my)):
            half = pl.ds(pl.multiple_of(y * HB, HB), HB)
            gn = dot(act_s[:, half], ol[...], 0, 0)
            gb = dot(low_s[:, half], nr[...], 0, 0)
            for t in range(T):
                rows = slice(t * HC, (t + 1) * HC)
                gs[2 * k + h, t % 2, t // 2, 0] = gn[rows, :].astype(BF16)
                gs[2 * k + h, t % 2, t // 2, 1] = gb[rows, :].astype(BF16)
            core_copy(2 * k + h).start()
        yacc[...] += dot(act_s[...], w2[cols, :], 1, 0)
        gacc[...] += dot(low_s[...], w1[:, cols], 1, 1)
        for h in range(2):
            i = 2 * k + h
            core_copy(i).wait_recv()
            for xx in range(2):
                for g in range(2):
                    add_into(gs.at[i, mc, xx, g], r1.at[i, xx, g])
            if h == 0:
                yq_copy(i).start()

            @pl.when(da == 1)
            def _():
                ar_copy(i).start()

            xp_copy(i).start()
        for at, ops in EARLY:

            @pl.when(k == at)
            def _():
                for op in ops:
                    take(*op)

        return carry

    lax.fori_loop(0, NDP // 2, block, 0)
    sent.extend([core_copy(i) for i in range(NDP)] + [xp_copy(i) for i in range(NDP)])
    sent.extend([yq_copy(i) for i, o in enumerate(ORDER) if o[0]] + [ar_copy(i) for i, o in enumerate(ORDER) if o[1]])
    for _, ops in EARLY:
        for op in ops:
            sent.extend(steps[op[0]](*op[1:])[-1])

    def ocopy(k, o, b):
        src, dst = (so, ro) if k == 0 else (so2, ro2)
        j = tpeer(o)
        return rc(src.at[j, OUT[b]], dst.at[te, OUT[b]], o_s.at[k, o - 1, b], o_r.at[k, o - 1, b], (dp, j))

    def ocopy_in(k, o, b):
        src, dst = (so, ro) if k == 0 else (so2, ro2)
        j = tpeer(o)
        return rc(src.at[j, OUT[b]], dst.at[j, OUT[b]], o_s.at[k, o - 1, b], o_r.at[k, o - 1, b], (dp, j))

    lc_o = [pltpu.make_async_copy(s.at[te], r.at[te], lsem.at[3 + k]) for k, (s, r) in enumerate(((so, ro), (so2, ro2)))]

    def pack(k, b, t, rows):
        dst = so if k == 0 else so2
        dst[t, IMG[b], :] = rows[0:PM, :].astype(BF16)
        tail = jnp.where(row8d == 0, rows[PM:PP, :], 0.0)
        if b == 0:
            ext[k, t] = tail
        else:
            dst[t, PM:PP, :] = (ext[k, t] + pltpu.roll(tail, 1, 0)).astype(BF16)

    def go(k, b):
        for o in (2, 3, 1):
            send(ocopy(k, o, b))
        if b == 1:
            lc_o[k].start()

    def part(b):
        return slice(b * half_r, (b + 1) * half_r)

    def lo(b):
        keep = jnp.where(2 * te + b < cnt[0], 1.0, 0.0)
        for t in range(T):
            sl = slice(b * half_r + t * PP, b * half_r + (t + 1) * PP)
            pack(0, b, t, (mixed[sl, :] + yacc[sl, :] + lowering) * keep)
        go(0, b)

    def ln2():
        resc_sum = jnp.zeros((1, D), F32)
        rece_sum = jnp.zeros((1, D), F32)
        for b in range(2):
            xh2, rs2 = norm_stats(mixed[part(b), :])
            gr = gacc[part(b), :]
            resc_sum = resc_sum + jnp.sum(gr * xh2, axis=0, keepdims=True)
            rece_sum = rece_sum + jnp.sum(gr, axis=0, keepdims=True)
            mgrad[part(b), :] = ol[part(b), :].astype(F32) + norm_back(gr, xh2, rs2, rescaling)
        vv[0, 2:3, 0:D] = resc_sum
        vv[0, 3:4, 0:D] = rece_sum

    hops = (x_dev, y_dev, a_dev, b_dev)
    e_core = rc(ec.at[1 - mc], ecr, e_s.at[0], e_r.at[0], core_dev)

    def v_copy(s):
        return rc(vv.at[s], vr.at[s], v_s.at[s], v_r.at[s], ((core_dev,) + hops)[s])

    def e_copy(s):
        return rc(es.at[s], er.at[s], e_s.at[s + 1], e_r.at[s + 1], hops[s])

    def tok():
        eg_sum = jnp.zeros((DS, PL), F32)
        cg_sum = jnp.zeros((DS + 8, PL), F32)
        for b in range(2):
            ml = mgrad[part(b), :].astype(BF16)
            _, slope = gelu_parts(tp[b])
            tg = (slope * dot(c_t, ml, 1, 0)).astype(BF16)
            tg16[b] = tg
            cg_sum = cg_sum + dot(ta[b], ml, 1, 1)
            eg_sum = eg_sum + dot(tg, nb16[part(b), :], 1, 1)
        vv[0, 5:6, 0:PL] = cg_sum[DS : DS + 1, :]
        for t in range(T):
            ec[t % 2, t // 2, 0] = eg_sum[t * DSL : (t + 1) * DSL, :]
            ec[t % 2, t // 2, 1] = cg_sum[t * DSL : (t + 1) * DSL, :]
        send(e_core)

    def f(b):
        nback = dot(e_clean, tg16[b], 0, 0)
        xhat, rs1 = norm_stats(image_rows(0, b))
        grad = mgrad[part(b), :] + norm_back(nback, xhat, rs1, scaling)
        for t in range(T):
            pack(1, b, t, grad[t * PP : (t + 1) * PP, :])
        sums[2 * b : 2 * b + 1, :] = jnp.sum(nback * xhat, axis=0, keepdims=True)
        sums[2 * b + 1 : 2 * b + 2, :] = jnp.sum(nback, axis=0, keepdims=True)

    def ig(b):
        go(1, b)

    def e(s):
        if s == 0:
            e_core.wait_recv()
            es[0] = (ec[mc, 1 - mx] + ecr[1 - mx]).astype(BF16)
            send(e_copy(0))
            return
        e_copy(s - 1).wait_recv()
        if s == 1:
            tot = ec[mc, mx] + ecr[mx] + er[0].astype(F32)
        else:
            tot = es[s - 1].astype(F32) + er[s - 1].astype(F32)
        if s == 4:
            ecf[...] = tot
        else:
            es[s] = tot.astype(BF16)
            send(e_copy(s))

    def v(s):
        if s == 0:
            for r in range(2):
                vv[0, r : r + 1, 0:D] = sums[r : r + 1, :] + sums[r + 2 : r + 3, :]
        else:
            v_copy(s - 1).wait_recv()
            vv[s] = vv[s - 1] + vr[s - 1]
        if s < 5:
            send(v_copy(s))

    work = dict(ln2=ln2, tok=tok, f=f, lo=lo, ig=ig, e=e, v=v)
    for op in LATE:
        if op[0] in work:
            work[op[0]](*op[1:])
        else:
            sent.extend(take(*op))

    for copy, rows, buf in ((bq_copy, QR, rbq), (br_copy, RR, rbr), (bp_copy, PR, rbp)):
        copy.wait_recv()
        for g in range(2):
            fin[g, rows, :] = gs[NDP - 1, mc, mx, g, rows, :].astype(F32) + buf[g].astype(F32)
    vec[...] = vv[5]
    for k in range(2):
        for o in (1, 2, 3):
            for b in range(2):
                ocopy_in(k, o, b).wait_recv()
        lc_o[k].wait()

    for c in sent:
        c.wait_send()


def finish_kernel(
    z, ro_h, ro2_h, fin_h, ecf_h, vec_h, lo, ig, eg, up, cg, off, v0, v1, v2, v3, bg, rg, ng, v4,
    xs, ro, ro2, ecf, vec, sem,
):
    D, PT, PP, HB, HC, T, NDP, DSL = z.D, z.PT, z.PP, z.HB, z.HC, z.T, z.NDP, z.DSL
    PM = PT - PT % 8
    te = lax.axis_index("tensor")
    di = lax.rem(lax.axis_index("dp"), NDP)
    pairs = ((ro_h, ro), (ro2_h, ro2), (ecf_h, ecf), (vec_h, vec), (fin_h.at[0], ng), (fin_h.at[1], bg))
    loads = [pltpu.make_async_copy(src, dst, sem.at[k]) for k, (src, dst) in enumerate(pairs)]
    for c in loads:
        c.start()
    for k, (src, dst) in enumerate(((ro, lo), (ro2, ig))):
        loads[k].wait()
        for c in range(D // LANES):
            lanes = slice(c * LANES, (c + 1) * LANES)
            base = c * PT * 8
            for j in range(T):
                for b, at in ((0, 0), (1, PP)):
                    xs[pl.ds(base + 2 * j + b, PM, stride=8), :] = src[j, at : at + PM, lanes].astype(F32)
                last = base + PM * 8 + 2 * j
                xs[last : last + 2, :] = src[j, PM:PP, lanes].astype(F32)[0:2, :]
            dst[:, :, lanes] = xs[base : base + PT * 8, :].reshape(PT, 8, LANES).astype(BF16)
    for c in loads[2:]:
        c.wait()
    pick = pick_matrix(T, PT, PP)
    eg[...] = dot_exact(ecf[0], pick, 1, 1)
    cg[...] = dot_exact(ecf[1], pick, 1, 1)
    row8 = lax.broadcasted_iota(jnp.int32, (8, PP * T), 1)
    up[...] = dot_exact(jnp.where(row8 == PT, 1.0, 0.0), ecf[0], 1, 1)[0:1, :].reshape(DSL)
    for ref, r in ((v0, 0), (v1, 1), (v2, 2), (v3, 3), (v4, 4)):
        ref[...] = vec[r : r + 1, 0:D].reshape(D)
    off_row = vec[5:6, :]
    rg_row = vec[pl.ds(di, 1), D:]
    off_own = jnp.zeros((1, PT), F32)
    rg_own = jnp.zeros((1, HC), F32)
    for t in range(T):
        off_own = off_own + jnp.where(te == t, off_row[:, t * PP : t * PP + PT], 0.0)
        rg_own = rg_own + jnp.where(te == t, rg_row[:, t * HC : (t + 1) * HC], 0.0)
    off[...] = off_own.reshape(PT)
    rg[...] = rg_own.reshape(HC)


def local(
    layer_input, image_counts, expand, uplift, contract, offset, scaling, centering,
    rescaling, recentering, broaden, raising, narrow, lowering, cotangent, *, mesh,
):
    z = Sizes()
    z.PT, images, z.D = layer_input.shape
    z.T, z.NDP = mesh.shape["tensor"], 8
    outer = mesh.shape["dp"] // z.NDP
    z.PP = -(-(z.PT + 1) // 8) * 8
    z.R = 2 * z.T * z.PP
    hidden = broaden.shape[1]
    if outer > 1:
        split = (outer, z.NDP, z.T, hidden // (outer * z.NDP * z.T))
        broaden = broaden.reshape(-1, *split).transpose(0, 2, 3, 1, 4).reshape(-1, hidden)
        raising = raising.reshape(split).transpose(1, 2, 0, 3).reshape(hidden)
        narrow = narrow.reshape(*split, -1).transpose(1, 2, 0, 3, 4).reshape(hidden, -1)
    z.HB = hidden // z.NDP
    z.HC = z.HB // z.T
    z.DSL = expand.shape[1]
    D, T, NDP, PP, PT, R, HB, HC, DSL = z.D, z.T, z.NDP, z.PP, z.PT, z.R, z.HB, z.HC, z.DSL
    DS, PL, PK = DSL * T, PP * T, PP + PT - PT % 8

    vm = pl.BlockSpec(memory_space=pltpu.VMEM)
    anys = pl.BlockSpec(memory_space=pl.ANY)
    dma = pltpu.SemaphoreType.DMA
    V = pltpu.VMEM
    S = jax.ShapeDtypeStruct
    z.P, z.Q = HC * 4 // 12, HC * 4 // 12
    P_, Q_, R_ = z.P, z.Q, HC - z.P - z.Q
    sems = []
    for shape in (
        (2, 3, 2), (8,), (NDP,), (NDP,), (4,), (2,), (), (4,), (2,), (2,), (), (4,), (2,), (2,), (),
        (2, 3, 2), (5,), (5,),
    ):
        sems += [dma(shape), dma(shape)]
    scratch = [
        V((PT, 8, D), BF16), V(broaden.shape, BF16), V(narrow.shape, BF16), V((D // LANES * PT * 8, LANES), F32),
        V((2, T, PK, D), BF16), V((2, T, PK, D), BF16), V((T, 2, DSL, PL), BF16), V((T, 8, PL), F32),
        V((R, D), BF16), V((2, DS, D), F32), V((2, DS + 8, D), BF16), V((R, D), F32), V((R, D), BF16), V((R, D), BF16),
        V((R, D), F32), V((R, D), F32), V((R, D), F32), V((NDP // 2, 2 * HB), F32), V((T, PK, D), BF16), V((T, PK, D), BF16),
        V((2, T, 8, D), F32), V((R, 2 * HB), BF16), V((R, 2 * HB), BF16), V((4, D), F32),
        V((NDP, 2, 2, 2, HC, D), BF16), V((NDP, 2, 2, HC, D), BF16),
        V((NDP, 2, P_, D), BF16), V((4, 2, P_, D), BF16), V((2, 2, P_, D), BF16), V((2, P_, D), BF16),
        V((4, 2, 2, Q_, D), BF16), V((2, 2, 2, Q_, D), BF16), V((2, 2, Q_, D), BF16), V((2, Q_, D), BF16),
        V((4, 2, 2, R_, D), BF16), V((2, 2, 2, R_, D), BF16), V((2, 2, R_, D), BF16), V((2, R_, D), BF16),
        V((6, 8, D + HB), F32), V((5, 8, D + HB), F32), V((2, 2, 2, DSL, PL), F32), V((2, 2, DSL, PL), F32),
        V((4, 2, DSL, PL), BF16), V((4, 2, DSL, PL), BF16), V((2, DS, D), BF16),
        dma((5,)),
    ] + sems
    mid = pl.pallas_call(
        functools.partial(layer_kernel, z),
        out_shape=(
            S((T, PK, D), BF16), S((T, PK, D), BF16), S((2, HC, D), F32), S((2, DSL, PL), F32), S((8, D + HB), F32),
        ),
        in_specs=[pl.BlockSpec(memory_space=pltpu.SMEM), vm, anys] + [vm] * 10 + [anys, anys],
        out_specs=(anys, anys, vm, vm, vm),
        scratch_shapes=scratch,
        compiler_params=pltpu.CompilerParams(
            collective_id=0, has_side_effects=True, vmem_limit_bytes=60 * 1024 * 1024
        ),
    )(
        image_counts, layer_input, cotangent, expand.T, contract, uplift, offset, scaling, centering,
        rescaling, recentering, lowering, raising, broaden, narrow,
    )
    res = pl.pallas_call(
        functools.partial(finish_kernel, z),
        out_shape=(
            S((PT, images, D), BF16), S((PT, images, D), BF16), S((DSL, PT * T), F32), S((DSL,), F32),
            S((DSL, PT * T), F32), S((PT,), F32), S((D,), F32), S((D,), F32), S((D,), F32), S((D,), F32),
            S((HC, D), F32), S((HC,), F32), S((HC, D), F32), S((D,), F32),
        ),
        in_specs=[anys] * 5,
        out_specs=(vm,) * 14,
        scratch_shapes=[
            V((D // LANES * PT * 8, LANES), F32), V((T, PK, D), BF16), V((T, PK, D), BF16), V((2, DSL, PL), F32),
            V((8, D + HB), F32), dma((6,)),
        ],
        compiler_params=pltpu.CompilerParams(vmem_limit_bytes=60 * 1024 * 1024),
    )(*mid)
    lo, ig, eg, up, cg, off, v0, v1, v2, v3, bg, rg, ng, v4 = res
    if outer > 1:
        same = [[o * NDP + i for o in range(outer)] for i in range(NDP)]
        eg, up, cg, off, v0, v1, v2, v3, v4 = lax.psum(
            (eg, up, cg, off, v0, v1, v2, v3, v4), "dp", axis_index_groups=same
        )
        bg, ng, rg = (
            lax.psum_scatter(v, "dp", scatter_dimension=0, axis_index_groups=same, tiled=True) for v in (bg, ng, rg)
        )
    return lo, ig, eg.T, up, cg, off, v0, v1, v2, v3, bg.T, rg, ng, v4


def solution(mesh):
    rows = P("tensor", "dp", None)
    both = ("dp", "tensor")
    in_specs = (
        rows, P("dp"), P(None, "tensor"), P("tensor"), P("tensor", None), P("tensor"),
        P(), P(), P(), P(), P(), P(), P(), P(), rows,
    )
    out_specs = (
        rows, rows, P(None, "tensor"), P("tensor"), P("tensor", None), P("tensor"),
        P(), P(), P(), P(), P(None, both), P(both), P(both, None), P(),
    )
    return jax.shard_map(
        functools.partial(local, mesh=mesh), mesh=mesh, in_specs=in_specs, out_specs=out_specs, check_vma=False
    )
```

```python
import functools

import jax
import jax.numpy as jnp
from jax import lax
from jax.experimental import pallas as pl
from jax.experimental.pallas import tpu as pltpu
from jax.sharding import PartitionSpec as P

MESH = pl.DeviceIdType.MESH
F32 = jnp.float32
BF16 = jnp.bfloat16
EPS = 1e-6
LANES = 128


def dot(a, b, ca, cb):
    return lax.dot_general(a, b, (((ca,), (cb,)), ((), ())), preferred_element_type=F32)


def dot_exact(a, b, ca, cb):
    return lax.dot_general(
        a, b, (((ca,), (cb,)), ((), ())), precision=lax.Precision.HIGHEST, preferred_element_type=F32
    )


def gelu_parts(v):
    c = 0.7978845608028654
    v2 = v * v
    t = jnp.tanh(c * v * (1.0 + 0.044715 * v2))
    half = 0.5 + 0.5 * t
    act = v * half
    slope = half + (0.5 * c) * v * (1.0 - t * t) * (1.0 + (3.0 * 0.044715) * v2)
    return act, slope


def norm_stats(v):
    cen = v - jnp.mean(v, axis=-1, keepdims=True)
    rs = lax.rsqrt(jnp.mean(cen * cen, axis=-1, keepdims=True) + EPS)
    return cen * rs, rs


def norm_back(grad, xhat, rs, gain):
    g = grad * gain
    return rs * (g - jnp.mean(g, axis=-1, keepdims=True) - xhat * jnp.mean(g * xhat, axis=-1, keepdims=True))


def pick_matrix(T, PT, PP):
    row = lax.broadcasted_iota(jnp.int32, (PT * T, PP * T), 0)
    col = lax.broadcasted_iota(jnp.int32, (PT * T, PP * T), 1)
    pick = jnp.zeros((PT * T, PP * T), F32)
    for t in range(T):
        inside = (col >= PP * t) & (col < PP * t + PT) & (row - PT * t == col - PP * t)
        pick = pick + jnp.where(inside, 1.0, 0.0)
    return pick


class Sizes:
    pass


ORDER = ((1, 1, 1), (0, 1, 1), (1, 0, 1), (0, 0, 1), (1, 1, 0), (0, 1, 0), (1, 0, 0), (0, 0, 0))

EARLY = (
    (2, (
        ("yq", 1, 1),
    )),
)
LATE = (
    ("lo", 0), ("xp", 1, 0, 1), ("yq", 0, 1), ("ln2",), ("ar", 1, 1), ("xp", 1, 1, 1), ("ar", 0, 1), ("aq", 1),
    ("tok",), ("f", 0), ("e", 0), ("af", 6), ("xp", 0, 0, 1), ("yq", 1, 0), ("f", 1), ("v", 0), ("xp", 0, 1, 1),
    ("v", 1), ("e", 1), ("xp", 0, 1, 0), ("xq", 1), ("yr", 1), ("yp", 0, 1), ("yp", 1, 1), ("lo", 1), ("af", 7),
    ("v", 2), ("ar", 0, 0), ("ar", 1, 0), ("yq", 0, 0), ("xr", 1), ("xp", 1, 1, 0), ("e", 2), ("xp", 1, 0, 0),
    ("ig", 0), ("ap", 1), ("v", 3), ("aq", 0), ("yr", 0), ("e", 3), ("ig", 1), ("v", 4), ("xp", 0, 0, 0),
    ("yp", 1, 0), ("yp", 0, 0), ("xq", 0), ("xr", 0), ("ap", 0), ("e", 4), ("v", 5),
)

def layer_kernel(
    z,
    cnt, x_hbm, ct_hbm, ex, co, uplift, offset, scal, cent, resc, rece, lowr, rais, w1_hbm, w2_hbm,
    ro, ro2, fin, ecf, vec,
    x, w1, w2, xs, sb, rb, et, cc, nb16, tp, ta, mixed, nr, ol, yacc, gacc, mgrad, bias, ext, act_s, slope_s, low_s, sums,
    gs, r1, rxp, ryp, rap, rbp, ryq, raq, rxq, rbq, rar, ryr, rxr, rbr,
    vv, vr, ec, ecr, es, er, tg16,
    lsem, a_s, a_r, w_s, w_r, c_s, c_r, xp_s, xp_r, yp_s, yp_r, ap_s, ap_r, bp_s, bp_r,
    yq_s, yq_r, aq_s, aq_r, xq_s, xq_r, bq_s, bq_r, ar_s, ar_r, yr_s, yr_r, xr_s, xr_r, br_s, br_r,
    o_s, o_r, v_s, v_r, e_s, e_r,
):
    D, PT, PP, R, HB, HC, T, NDP = z.D, z.PT, z.PP, z.R, z.HB, z.HC, z.T, z.NDP
    DSL, DS = z.DSL, z.DSL * T
    PL = PP * T
    half_r = R // 2
    dp = lax.axis_index("dp")
    te = lax.axis_index("tensor")
    di = lax.rem(dp, NDP)
    mc = lax.rem(te, 2)
    mx = te // 2
    my = lax.rem(di, 2)
    mz = di // 2

    def tpeer(o):
        if o == 1:
            return te + 1 - 2 * mc
        if o == 2:
            return lax.rem(te + 2, 4)
        return 3 - te

    core_dev = (dp, tpeer(1))
    x_dev = (dp, tpeer(2))
    y_dev = (dp + 1 - 2 * my, te)

    a_dev = (dp + 2 - 4 * lax.rem(mz, 2), te)
    b_dev = (dp - di + lax.rem(di + 4, NDP), te)
    ma, mb = lax.rem(mz, 2), mz // 2

    def rc(src, dst, ss, rs, dev):
        return pltpu.make_async_remote_copy(
            src_ref=src, dst_ref=dst, send_sem=ss, recv_sem=rs, device_id=dev, device_id_type=MESH
        )

    sent = []

    def send(copy):
        copy.start()
        sent.append(copy)

    lc_ct = pltpu.make_async_copy(ct_hbm, x, lsem.at[0])
    lc_w1 = pltpu.make_async_copy(w1_hbm, w1, lsem.at[1])
    lc_w2 = pltpu.make_async_copy(w2_hbm, w2, lsem.at[2])
    lc_x = pltpu.make_async_copy(x_hbm, x, lsem.at[5])
    lc_x.start()

    peers = [(dp, tpeer(o)) for o in (1, 2, 3)] + [y_dev, a_dev, b_dev]
    bar = pltpu.get_barrier_semaphore()
    for dev in peers:
        pl.semaphore_signal(bar, inc=1, device_id=dev, device_id_type=MESH)

    row8 = lax.broadcasted_iota(jnp.int32, (8, LANES), 0)
    PM = PT - PT % 8
    IMG = (slice(0, PM), slice(PP, PP + PM))
    IN = (pl.ds(0, PP), pl.ds(PP, PM))
    OUT = (pl.ds(0, PM), pl.ds(PM, PP))

    def spread(src, k):
        for c in range(D // LANES):
            lanes = slice(c * LANES, (c + 1) * LANES)
            base = c * PT * 8
            xs[base : base + PT * 8, :] = src[:, :, lanes].astype(F32).reshape(PT * 8, LANES)
            tail = xs[base + PM * 8 : base + PT * 8, :]
            for j in range(T):
                for b in range(2):
                    sb[k, j, IMG[b], lanes] = xs[pl.ds(base + 2 * j + b, PM, stride=8), :].astype(BF16)
                two = tail if j == 0 else pltpu.roll(tail, 8 - 2 * j, 0)
                sb[k, j, PM:PP, lanes] = jnp.where(row8 < 2, two, 0.0).astype(BF16)

    def a2a(k, o, b):
        j = tpeer(o)
        return rc(sb.at[k, j, IN[b]], rb.at[k, te, IN[b]], a_s.at[k, o - 1, b], a_r.at[k, o - 1, b], (dp, j))

    def a2a_in(k, o, b):
        j = tpeer(o)
        return rc(sb.at[k, j, IN[b]], rb.at[k, j, IN[b]], a_s.at[k, o - 1, b], a_r.at[k, o - 1, b], (dp, j))

    lc_x.wait()
    spread(x, 0)
    lc_ct.start()
    pl.semaphore_wait(bar, len(peers))
    for o in (2, 3, 1):
        a2a(0, o, 0).start()

    pick = pick_matrix(T, PT, PP)
    pick16 = pick.astype(BF16)
    col1 = lax.broadcasted_iota(jnp.int32, (1, PL), 1)
    pad_one = jnp.where(col1 == PT, 1.0, 0.0)
    uplift_col = dot_exact(uplift[...].astype(F32).reshape(1, DSL), pad_one, 0, 0)
    et[te, 0] = (dot(ex[...], pick16, 1, 0) + uplift_col).astype(BF16)
    et[te, 1] = dot(co[...], pick16, 1, 0).astype(BF16)
    off_line = offset[...].astype(F32).reshape(1, PT)
    own_cols = (lax.broadcasted_iota(jnp.int32, (PT, PL), 1) - PP * te) == lax.broadcasted_iota(
        jnp.int32, (PT, PL), 0
    )
    off_row = dot(off_line.astype(BF16), jnp.where(own_cols, 1.0, 0.0).astype(BF16), 1, 0)
    cc[te] = jnp.broadcast_to(off_row, (8, PL))

    tx, t3 = tpeer(2), tpeer(3)

    def wcopy(k, ref, dev):
        return rc(ref, ref, w_s.at[k], w_r.at[k], dev)

    send(wcopy(0, et.at[te, my], x_dev))
    send(wcopy(1, cc.at[te], x_dev))
    for o in (2, 3, 1):
        a2a(0, o, 1).start()
    send(wcopy(2, et.at[te], core_dev))
    send(wcopy(3, cc.at[te], core_dev))
    rb[0, te] = sb[0, te]

    lc_ct.wait()
    lc_w1.start()
    lc_w2.start()
    spread(x, 1)
    for b in range(2):
        for o in (2, 3, 1):
            a2a(1, o, b).start()
    rb[1, te] = sb[1, te]

    wcopy(0, et.at[tx, my], x_dev).wait_recv()
    send(wcopy(4, et.at[tx, my], y_dev))
    wcopy(1, cc.at[tx], x_dev).wait_recv()
    send(wcopy(5, et.at[tx, my], core_dev))
    send(wcopy(6, cc.at[tx], core_dev))
    bias_line = rais[...].astype(F32).reshape(1, HB * NDP)
    for m in range(NDP // 2):
        bias[m : m + 1, :] = bias_line[:, 2 * m * HB : 2 * (m + 1) * HB]
    scaling, centering = scal[...].astype(F32).reshape(1, D), cent[...].astype(F32).reshape(1, D)
    rescaling, recentering = resc[...].astype(F32).reshape(1, D), rece[...].astype(F32).reshape(1, D)
    lowering = lowr[...].astype(F32).reshape(1, D)
    wcopy(4, et.at[tx, 1 - my], y_dev).wait_recv()
    send(wcopy(7, et.at[tx, 1 - my], core_dev))
    tc = tpeer(1)
    for k, ref in ((2, et.at[tc]), (3, cc.at[tc]), (5, et.at[t3, my]), (6, cc.at[t3]), (7, et.at[t3, 1 - my])):
        wcopy(k, ref, core_dev).wait_recv()

    e_t = et[:, 0].reshape(DS, PL)
    c_t = et[:, 1].reshape(DS, PL)
    zero_pad = lax.broadcasted_iota(jnp.int32, (DS, PL), 1) == PT
    e_clean = jnp.where(zero_pad, 0.0, e_t.astype(F32)).astype(BF16)
    off_full = (cc[0] + cc[1]) + (cc[2] + cc[3])
    first8 = lax.broadcasted_iota(jnp.int32, (8, PL), 0) == 0
    off_row8 = jnp.where(first8, off_full, 0.0).astype(BF16)
    ones_row = lax.broadcasted_iota(jnp.int32, (half_r, 1), 0) == PT
    row8d = lax.broadcasted_iota(jnp.int32, (8, D), 0)
    ones8 = jnp.where(row8d == 0, 1.0, 0.0).astype(BF16)

    def image_rows(k, b):
        pieces = []
        for t in range(T):
            tail = rb[k, t, PM:PP, :].astype(F32)
            tail = pltpu.roll(tail, 7, 0) if b else tail
            pieces += [rb[k, t, IMG[b], :].astype(F32), jnp.where(row8d == 0, tail, 0.0)]
        return jnp.concatenate(pieces, axis=0)

    for b in range(2):
        for o in (1, 2, 3):
            a2a_in(0, o, b).wait_recv()
        sl = slice(b * half_r, (b + 1) * half_r)
        xb = image_rows(0, b)
        xhat, _ = norm_stats(xb)
        n = jnp.where(ones_row, 1.0, xhat * scaling + centering).astype(BF16)
        nb16[sl, :] = n
        pre = dot(e_t, n, 1, 0)
        tp[b] = pre
        act, _ = gelu_parts(pre)
        ta[b, 0:DS, :] = act.astype(BF16)
        ta[b, DS : DS + 8, :] = ones8
        mx_b = xb + dot(c_t, ta[b, 0:DS, :], 0, 0) + dot(off_row8, ones8, 0, 0)
        mixed[sl, :] = mx_b
        xh2, _ = norm_stats(mx_b)
        nr[sl, :] = (xh2 * rescaling + recentering).astype(BF16)

    def flip(m, bit):
        return m + bit - 2 * m * bit

    def pair(k):
        m = flip(mb, 1 - k // 2) * 2 + flip(ma, 1 - k % 2)
        return m, pl.ds(pl.multiple_of(m * 2 * HB, 2 * HB), 2 * HB)

    def ahead(k):
        m, cols = pair(k)
        act, slope = gelu_parts(dot(nr[...], w1[:, cols], 1, 0) + bias[pl.ds(m, 1), :])
        act_s[...] = act.astype(BF16)
        slope_s[...] = slope

    yacc[...] = jnp.zeros(yacc.shape, F32)
    gacc[...] = jnp.zeros(gacc.shape, F32)
    vv[0] = jnp.zeros(vv.shape[1:], F32)
    lc_w1.wait()
    lc_w2.wait()
    ahead(0)
    low_sum = jnp.zeros((1, D), F32)
    for b in range(2):
        for o in (1, 2, 3):
            a2a_in(1, o, b).wait_recv()
        sl = slice(b * half_r, (b + 1) * half_r)
        keep = jnp.where(2 * te + b < cnt[0], 1.0, 0.0)
        og = image_rows(1, b) * keep
        ol[sl, :] = og.astype(BF16)
        low_sum = low_sum + jnp.sum(og, axis=0, keepdims=True)
    vv[0, 4:5, 0:D] = low_sum

    PR, QR, RR = pl.ds(0, z.P), pl.ds(z.P, z.Q), pl.ds(z.P + z.Q, HC - z.P - z.Q)
    pos = {o: i for i, o in enumerate(ORDER)}

    def add_into(dst, src):
        dst[...] = (dst[...].astype(F32) + src[...].astype(F32)).astype(BF16)

    def piece(o, rows, xx):
        if xx is None:
            return gs.at[pos[o], mc, :, :, rows]
        return gs.at[pos[o], mc, xx, :, rows]

    def core_copy(i):
        return rc(gs.at[i, 1 - mc], r1.at[i], c_s.at[i], c_r.at[i], core_dev)

    def xp_copy(i):
        return rc(gs.at[i, mc, 1 - mx, :, PR], rxp.at[i], xp_s.at[i], xp_r.at[i], x_dev)

    def yq_copy(i):
        k = i // 2
        return rc(gs.at[i, mc, :, :, QR], ryq.at[k], yq_s.at[k], yq_r.at[k], y_dev)

    def ar_copy(i):
        k = i // 4 * 2 + i % 2
        return rc(gs.at[i, mc, :, :, RR], rar.at[k], ar_s.at[k], ar_r.at[k], a_dev)

    def yp_copy(da, db):
        k = 2 * da + db
        return rc(piece((1, da, db), PR, mx), ryp.at[k], yp_s.at[k], yp_r.at[k], y_dev)

    def ap_copy(db):
        return rc(piece((0, 1, db), PR, mx), rap.at[db], ap_s.at[db], ap_r.at[db], a_dev)

    def aq_copy(db):
        return rc(piece((0, 1, db), QR, None), raq.at[db], aq_s.at[db], aq_r.at[db], a_dev)

    def xq_copy(db):
        return rc(piece((0, 0, db), QR, 1 - mx), rxq.at[db], xq_s.at[db], xq_r.at[db], x_dev)

    def yr_copy(db):
        return rc(piece((1, 0, db), RR, None), ryr.at[db], yr_s.at[db], yr_r.at[db], y_dev)

    def xr_copy(db):
        return rc(piece((0, 0, db), RR, 1 - mx), rxr.at[db], xr_s.at[db], xr_r.at[db], x_dev)

    bp_copy = rc(piece((0, 0, 1), PR, mx), rbp, bp_s, bp_r, b_dev)
    bq_copy = rc(piece((0, 0, 1), QR, mx), rbq, bq_s, bq_r, b_dev)
    br_copy = rc(piece((0, 0, 1), RR, mx), rbr, br_s, br_r, b_dev)

    def xp(dy, da, db):
        o = (dy, da, db)
        return xp_copy(pos[o]), o, PR, rxp.at[pos[o]], False, [yp_copy(da, db)] if dy else []

    def yp(da, db):
        return yp_copy(da, db), (0, da, db), PR, ryp.at[2 * da + db], False, [ap_copy(db)] if da else []

    def ap(db):
        return ap_copy(db), (0, 0, db), PR, rap.at[db], False, [bp_copy] if db else []

    def yq(da, db):
        i = pos[1, da, db]
        return yq_copy(i), (0, da, db), QR, ryq.at[i // 2], True, [aq_copy(db)] if da else []

    def aq(db):
        return aq_copy(db), (0, 0, db), QR, raq.at[db], True, [xq_copy(db)]

    def xq(db):
        return xq_copy(db), (0, 0, db), QR, rxq.at[db], False, [bq_copy] if db else []

    def ar(dy, db):
        i = pos[dy, 1, db]
        return ar_copy(i), (dy, 0, db), RR, rar.at[i // 4 * 2 + i % 2], True, [yr_copy(db)] if dy else []

    def yr(db):
        return yr_copy(db), (0, 0, db), RR, ryr.at[db], True, [xr_copy(db)]

    def xr(db):
        return xr_copy(db), (0, 0, db), RR, rxr.at[db], False, [br_copy] if db else []

    steps = dict(xp=xp, yp=yp, ap=ap, yq=yq, aq=aq, xq=xq, ar=ar, yr=yr, xr=xr)

    def take(name, *bits):
        arrival, o, rows, src, both, on = steps[name](*bits)
        arrival.wait_recv()
        for g in range(2):
            if both:
                for xx in range(2):
                    add_into(gs.at[pos[o], mc, xx, g, rows], src.at[xx, g])
            else:
                add_into(gs.at[pos[o], mc, mx, g, rows], src.at[g])
        for c in on:
            c.start()
        return on

    def af(i):
        core_copy(i).wait_recv()
        for xx in range(2):
            for g in range(2):
                add_into(gs.at[i, mc, xx, g], r1.at[i, xx, g])

    def first_hops(i):
        dy, da, _ = ORDER[i]
        if dy:
            yq_copy(i).start()
        if da:
            ar_copy(i).start()
        xp_copy(i).start()

    for k in range(NDP // 2):
        m, cols = pair(k)
        low16 = (slope_s[...] * dot(ol[...], w2[cols, :], 1, 1)).astype(BF16)
        low_s[...] = low16
        line = jnp.sum(low16.astype(F32), axis=0, keepdims=True)
        for y in range(2):
            vv[0, pl.ds(2 * m + y, 1), D : D + HB] = line[:, y * HB : (y + 1) * HB]
        if k > 0:
            for i in (2 * k - 2, 2 * k - 1):
                af(i)
                first_hops(i)
        gn = dot(act_s[...], ol[...], 0, 0)
        gb = dot(low_s[...], nr[...], 0, 0)
        for y, h in ((0, 1 - my), (1, my)):
            for t in range(T):
                rows = slice(y * HB + t * HC, y * HB + (t + 1) * HC)
                gs[2 * k + h, t % 2, t // 2, 0] = gn[rows, :].astype(BF16)
                gs[2 * k + h, t % 2, t // 2, 1] = gb[rows, :].astype(BF16)
        for h in range(2):
            core_copy(2 * k + h).start()
        yacc[...] += dot(act_s[...], w2[cols, :], 1, 0)
        gacc[...] += dot(low_s[...], w1[:, cols], 1, 1)
        if k + 1 < NDP // 2:
            ahead(k + 1)
        for at, ops in EARLY:
            if at == k:
                for op in ops:
                    take(*op)

    sent.extend([core_copy(i) for i in range(NDP)] + [xp_copy(i) for i in range(NDP)])
    sent.extend([yq_copy(i) for i, o in enumerate(ORDER) if o[0]] + [ar_copy(i) for i, o in enumerate(ORDER) if o[1]])
    for _, ops in EARLY:
        for op in ops:
            sent.extend(steps[op[0]](*op[1:])[-1])

    so, so2 = sb.at[0], sb.at[1]
    for k in range(2):
        for o in (1, 2, 3):
            for b in range(2):
                a2a(k, o, b).wait_send()

    def ocopy(k, o, b):
        src, dst = (so, ro) if k == 0 else (so2, ro2)
        j = tpeer(o)
        return rc(src.at[j, OUT[b]], dst.at[te, OUT[b]], o_s.at[k, o - 1, b], o_r.at[k, o - 1, b], (dp, j))

    def ocopy_in(k, o, b):
        src, dst = (so, ro) if k == 0 else (so2, ro2)
        j = tpeer(o)
        return rc(src.at[j, OUT[b]], dst.at[j, OUT[b]], o_s.at[k, o - 1, b], o_r.at[k, o - 1, b], (dp, j))

    lc_o = [pltpu.make_async_copy(s.at[te], r.at[te], lsem.at[3 + k]) for k, (s, r) in enumerate(((so, ro), (so2, ro2)))]

    def pack(k, b, t, rows):
        dst = so if k == 0 else so2
        dst[t, IMG[b], :] = rows[0:PM, :].astype(BF16)
        tail = jnp.where(row8d == 0, rows[PM:PP, :], 0.0)
        if b == 0:
            ext[k, t] = tail
        else:
            dst[t, PM:PP, :] = (ext[k, t] + pltpu.roll(tail, 1, 0)).astype(BF16)

    def go(k, b):
        for o in (2, 3, 1):
            send(ocopy(k, o, b))
        if b == 1:
            lc_o[k].start()

    def part(b):
        return slice(b * half_r, (b + 1) * half_r)

    def lo(b):
        keep = jnp.where(2 * te + b < cnt[0], 1.0, 0.0)
        for t in range(T):
            sl = slice(b * half_r + t * PP, b * half_r + (t + 1) * PP)
            pack(0, b, t, (mixed[sl, :] + yacc[sl, :] + lowering) * keep)
        go(0, b)

    def ln2():
        resc_sum = jnp.zeros((1, D), F32)
        rece_sum = jnp.zeros((1, D), F32)
        for b in range(2):
            xh2, rs2 = norm_stats(mixed[part(b), :])
            gr = gacc[part(b), :]
            resc_sum = resc_sum + jnp.sum(gr * xh2, axis=0, keepdims=True)
            rece_sum = rece_sum + jnp.sum(gr, axis=0, keepdims=True)
            mgrad[part(b), :] = ol[part(b), :].astype(F32) + norm_back(gr, xh2, rs2, rescaling)
        vv[0, 2:3, 0:D] = resc_sum
        vv[0, 3:4, 0:D] = rece_sum

    hops = (x_dev, y_dev, a_dev, b_dev)
    e_core = rc(ec.at[1 - mc], ecr, e_s.at[0], e_r.at[0], core_dev)

    def v_copy(s):
        return rc(vv.at[s], vr.at[s], v_s.at[s], v_r.at[s], ((core_dev,) + hops)[s])

    def e_copy(s):
        return rc(es.at[s], er.at[s], e_s.at[s + 1], e_r.at[s + 1], hops[s])

    def tok():
        eg_sum = jnp.zeros((DS, PL), F32)
        cg_sum = jnp.zeros((DS + 8, PL), F32)
        for b in range(2):
            ml = mgrad[part(b), :].astype(BF16)
            _, slope = gelu_parts(tp[b])
            tg = (slope * dot(c_t, ml, 1, 0)).astype(BF16)
            tg16[b] = tg
            cg_sum = cg_sum + dot(ta[b], ml, 1, 1)
            eg_sum = eg_sum + dot(tg, nb16[part(b), :], 1, 1)
        vv[0, 5:6, 0:PL] = cg_sum[DS : DS + 1, :]
        for t in range(T):
            ec[t % 2, t // 2, 0] = eg_sum[t * DSL : (t + 1) * DSL, :]
            ec[t % 2, t // 2, 1] = cg_sum[t * DSL : (t + 1) * DSL, :]
        send(e_core)

    def f(b):
        nback = dot(e_clean, tg16[b], 0, 0)
        xhat, rs1 = norm_stats(image_rows(0, b))
        grad = mgrad[part(b), :] + norm_back(nback, xhat, rs1, scaling)
        for t in range(T):
            pack(1, b, t, grad[t * PP : (t + 1) * PP, :])
        sums[2 * b : 2 * b + 1, :] = jnp.sum(nback * xhat, axis=0, keepdims=True)
        sums[2 * b + 1 : 2 * b + 2, :] = jnp.sum(nback, axis=0, keepdims=True)

    def ig(b):
        go(1, b)

    def e(s):
        if s == 0:
            e_core.wait_recv()
            es[0] = (ec[mc, 1 - mx] + ecr[1 - mx]).astype(BF16)
            send(e_copy(0))
            return
        e_copy(s - 1).wait_recv()
        if s == 1:
            tot = ec[mc, mx] + ecr[mx] + er[0].astype(F32)
        else:
            tot = es[s - 1].astype(F32) + er[s - 1].astype(F32)
        if s == 4:
            ecf[...] = tot
        else:
            es[s] = tot.astype(BF16)
            send(e_copy(s))

    def v(s):
        if s == 0:
            for r in range(2):
                vv[0, r : r + 1, 0:D] = sums[r : r + 1, :] + sums[r + 2 : r + 3, :]
        else:
            v_copy(s - 1).wait_recv()
            vv[s] = vv[s - 1] + vr[s - 1]
        if s < 5:
            send(v_copy(s))

    def last_block(i):
        af(i)
        first_hops(i)

    work = dict(af=last_block, ln2=ln2, tok=tok, f=f, lo=lo, ig=ig, e=e, v=v)
    for op in LATE:
        if op[0] in work:
            work[op[0]](*op[1:])
        else:
            sent.extend(take(*op))

    for copy, rows, buf in ((bq_copy, QR, rbq), (br_copy, RR, rbr), (bp_copy, PR, rbp)):
        copy.wait_recv()
        for g in range(2):
            fin[g, rows, :] = gs[NDP - 1, mc, mx, g, rows, :].astype(F32) + buf[g].astype(F32)
    vec[...] = vv[5]
    for k in range(2):
        for o in (1, 2, 3):
            for b in range(2):
                ocopy_in(k, o, b).wait_recv()
        lc_o[k].wait()

    for c in sent:
        c.wait_send()


def finish_kernel(
    z, ro_h, ro2_h, fin_h, ecf_h, vec_h, lo, ig, eg, up, cg, off, v0, v1, v2, v3, bg, rg, ng, v4,
    xs, ro, ro2, ecf, vec, sem,
):
    D, PT, PP, HB, HC, T, NDP, DSL = z.D, z.PT, z.PP, z.HB, z.HC, z.T, z.NDP, z.DSL
    PM = PT - PT % 8
    te = lax.axis_index("tensor")
    di = lax.rem(lax.axis_index("dp"), NDP)
    pairs = ((ro_h, ro), (ro2_h, ro2), (ecf_h, ecf), (vec_h, vec), (fin_h.at[0], ng), (fin_h.at[1], bg))
    loads = [pltpu.make_async_copy(src, dst, sem.at[k]) for k, (src, dst) in enumerate(pairs)]
    for c in loads:
        c.start()
    for k, (src, dst) in enumerate(((ro, lo), (ro2, ig))):
        loads[k].wait()
        for c in range(D // LANES):
            lanes = slice(c * LANES, (c + 1) * LANES)
            base = c * PT * 8
            for j in range(T):
                for b, at in ((0, 0), (1, PP)):
                    xs[pl.ds(base + 2 * j + b, PM, stride=8), :] = src[j, at : at + PM, lanes].astype(F32)
                last = base + PM * 8 + 2 * j
                xs[last : last + 2, :] = src[j, PM:PP, lanes].astype(F32)[0:2, :]
            dst[:, :, lanes] = xs[base : base + PT * 8, :].reshape(PT, 8, LANES).astype(BF16)
    for c in loads[2:]:
        c.wait()
    pick = pick_matrix(T, PT, PP)
    eg[...] = dot_exact(ecf[0], pick, 1, 1)
    cg[...] = dot_exact(ecf[1], pick, 1, 1)
    row8 = lax.broadcasted_iota(jnp.int32, (8, PP * T), 1)
    up[...] = dot_exact(jnp.where(row8 == PT, 1.0, 0.0), ecf[0], 1, 1)[0:1, :].reshape(DSL)
    for ref, r in ((v0, 0), (v1, 1), (v2, 2), (v3, 3), (v4, 4)):
        ref[...] = vec[r : r + 1, 0:D].reshape(D)
    off_row = vec[5:6, :]
    rg_row = vec[pl.ds(di, 1), D:]
    off_own = jnp.zeros((1, PT), F32)
    rg_own = jnp.zeros((1, HC), F32)
    for t in range(T):
        off_own = off_own + jnp.where(te == t, off_row[:, t * PP : t * PP + PT], 0.0)
        rg_own = rg_own + jnp.where(te == t, rg_row[:, t * HC : (t + 1) * HC], 0.0)
    off[...] = off_own.reshape(PT)
    rg[...] = rg_own.reshape(HC)


def local(
    layer_input, image_counts, expand, uplift, contract, offset, scaling, centering,
    rescaling, recentering, broaden, raising, narrow, lowering, cotangent, *, mesh,
):
    z = Sizes()
    z.PT, images, z.D = layer_input.shape
    z.T, z.NDP = mesh.shape["tensor"], 8
    outer = mesh.shape["dp"] // z.NDP
    z.PP = -(-(z.PT + 1) // 8) * 8
    z.R = 2 * z.T * z.PP
    hidden = broaden.shape[1]
    if outer > 1:
        split = (outer, z.NDP, z.T, hidden // (outer * z.NDP * z.T))
        broaden = broaden.reshape(-1, *split).transpose(0, 2, 3, 1, 4).reshape(-1, hidden)
        raising = raising.reshape(split).transpose(1, 2, 0, 3).reshape(hidden)
        narrow = narrow.reshape(*split, -1).transpose(1, 2, 0, 3, 4).reshape(hidden, -1)
    z.HB = hidden // z.NDP
    z.HC = z.HB // z.T
    z.DSL = expand.shape[1]
    D, T, NDP, PP, PT, R, HB, HC, DSL = z.D, z.T, z.NDP, z.PP, z.PT, z.R, z.HB, z.HC, z.DSL
    DS, PL, PK = DSL * T, PP * T, PP + PT - PT % 8

    vm = pl.BlockSpec(memory_space=pltpu.VMEM)
    anys = pl.BlockSpec(memory_space=pl.ANY)
    dma = pltpu.SemaphoreType.DMA
    V = pltpu.VMEM
    S = jax.ShapeDtypeStruct
    z.P, z.Q = HC * 4 // 12, HC * 4 // 12
    P_, Q_, R_ = z.P, z.Q, HC - z.P - z.Q
    sems = []
    for shape in (
        (2, 3, 2), (8,), (NDP,), (NDP,), (4,), (2,), (), (4,), (2,), (2,), (), (4,), (2,), (2,), (),
        (2, 3, 2), (5,), (5,),
    ):
        sems += [dma(shape), dma(shape)]
    scratch = [
        V((PT, 8, D), BF16), V(broaden.shape, BF16), V(narrow.shape, BF16), V((D // LANES * PT * 8, LANES), F32),
        V((2, T, PK, D), BF16), V((2, T, PK, D), BF16), V((T, 2, DSL, PL), BF16), V((T, 8, PL), F32),
        V((R, D), BF16), V((2, DS, D), F32), V((2, DS + 8, D), BF16), V((R, D), F32), V((R, D), BF16), V((R, D), BF16),
        V((R, D), F32), V((R, D), F32), V((R, D), F32), V((NDP // 2, 2 * HB), F32),
        V((2, T, 8, D), F32), V((R, 2 * HB), BF16), V((R, 2 * HB), F32), V((R, 2 * HB), BF16), V((4, D), F32),
        V((NDP, 2, 2, 2, HC, D), BF16), V((NDP, 2, 2, HC, D), BF16),
        V((NDP, 2, P_, D), BF16), V((4, 2, P_, D), BF16), V((2, 2, P_, D), BF16), V((2, P_, D), BF16),
        V((4, 2, 2, Q_, D), BF16), V((2, 2, 2, Q_, D), BF16), V((2, 2, Q_, D), BF16), V((2, Q_, D), BF16),
        V((4, 2, 2, R_, D), BF16), V((2, 2, 2, R_, D), BF16), V((2, 2, R_, D), BF16), V((2, R_, D), BF16),
        V((6, 8, D + HB), F32), V((5, 8, D + HB), F32), V((2, 2, 2, DSL, PL), F32), V((2, 2, DSL, PL), F32),
        V((4, 2, DSL, PL), BF16), V((4, 2, DSL, PL), BF16), V((2, DS, D), BF16),
        dma((6,)),
    ] + sems
    mid = pl.pallas_call(
        functools.partial(layer_kernel, z),
        out_shape=(
            S((T, PK, D), BF16), S((T, PK, D), BF16), S((2, HC, D), F32), S((2, DSL, PL), F32), S((8, D + HB), F32),
        ),
        in_specs=[pl.BlockSpec(memory_space=pltpu.SMEM), anys, anys] + [vm] * 10 + [anys, anys],
        out_specs=(anys, anys, vm, vm, vm),
        scratch_shapes=scratch,
        compiler_params=pltpu.CompilerParams(
            collective_id=0, has_side_effects=True, vmem_limit_bytes=62 * 1024 * 1024
        ),
    )(
        image_counts, layer_input, cotangent, expand.T, contract, uplift, offset, scaling, centering,
        rescaling, recentering, lowering, raising, broaden, narrow,
    )
    res = pl.pallas_call(
        functools.partial(finish_kernel, z),
        out_shape=(
            S((PT, images, D), BF16), S((PT, images, D), BF16), S((DSL, PT * T), F32), S((DSL,), F32),
            S((DSL, PT * T), F32), S((PT,), F32), S((D,), F32), S((D,), F32), S((D,), F32), S((D,), F32),
            S((HC, D), F32), S((HC,), F32), S((HC, D), F32), S((D,), F32),
        ),
        in_specs=[anys] * 5,
        out_specs=(vm,) * 14,
        scratch_shapes=[
            V((D // LANES * PT * 8, LANES), F32), V((T, PK, D), BF16), V((T, PK, D), BF16), V((2, DSL, PL), F32),
            V((8, D + HB), F32), dma((6,)),
        ],
        compiler_params=pltpu.CompilerParams(vmem_limit_bytes=60 * 1024 * 1024),
    )(*mid)
    lo, ig, eg, up, cg, off, v0, v1, v2, v3, bg, rg, ng, v4 = res
    if outer > 1:
        same = [[o * NDP + i for o in range(outer)] for i in range(NDP)]
        eg, up, cg, off, v0, v1, v2, v3, v4 = lax.psum(
            (eg, up, cg, off, v0, v1, v2, v3, v4), "dp", axis_index_groups=same
        )
        bg, ng, rg = (
            lax.psum_scatter(v, "dp", scatter_dimension=0, axis_index_groups=same, tiled=True) for v in (bg, ng, rg)
        )
    return lo, ig, eg.T, up, cg, off, v0, v1, v2, v3, bg.T, rg, ng, v4


def solution(mesh):
    rows = P("tensor", "dp", None)
    both = ("dp", "tensor")
    in_specs = (
        rows, P("dp"), P(None, "tensor"), P("tensor"), P("tensor", None), P("tensor"),
        P(), P(), P(), P(), P(), P(), P(), P(), rows,
    )
    out_specs = (
        rows, rows, P(None, "tensor"), P("tensor"), P("tensor", None), P("tensor"),
        P(), P(), P(), P(), P(None, both), P(both), P(both, None), P(),
    )
    return jax.shard_map(
        functools.partial(local, mesh=mesh), mesh=mesh, in_specs=in_specs, out_specs=out_specs, check_vma=False
    )
```

```python
import functools

import jax
import jax.numpy as jnp
from jax import lax
from jax.experimental import pallas as pl
from jax.experimental.pallas import tpu as pltpu
from jax.sharding import PartitionSpec as P

MESH = pl.DeviceIdType.MESH
F32 = jnp.float32
BF16 = jnp.bfloat16
EPS = 1e-6
LANES = 128


def dot(a, b, ca, cb):
    return lax.dot_general(a, b, (((ca,), (cb,)), ((), ())), preferred_element_type=F32)


def dot_exact(a, b, ca, cb):
    return lax.dot_general(
        a, b, (((ca,), (cb,)), ((), ())), precision=lax.Precision.HIGHEST, preferred_element_type=F32
    )


def gelu_parts(v):
    c = 0.7978845608028654
    v2 = v * v
    t = jnp.tanh(c * v * (1.0 + 0.044715 * v2))
    half = 0.5 + 0.5 * t
    act = v * half
    slope = half + (0.5 * c) * v * (1.0 - t * t) * (1.0 + (3.0 * 0.044715) * v2)
    return act, slope


def norm_stats(v):
    cen = v - jnp.mean(v, axis=-1, keepdims=True)
    rs = lax.rsqrt(jnp.mean(cen * cen, axis=-1, keepdims=True) + EPS)
    return cen * rs, rs


def norm_back(grad, xhat, rs, gain):
    g = grad * gain
    return rs * (g - jnp.mean(g, axis=-1, keepdims=True) - xhat * jnp.mean(g * xhat, axis=-1, keepdims=True))


def pick_matrix(T, PT, PP):
    row = lax.broadcasted_iota(jnp.int32, (PT * T, PP * T), 0)
    col = lax.broadcasted_iota(jnp.int32, (PT * T, PP * T), 1)
    pick = jnp.zeros((PT * T, PP * T), F32)
    for t in range(T):
        inside = (col >= PP * t) & (col < PP * t + PT) & (row - PT * t == col - PP * t)
        pick = pick + jnp.where(inside, 1.0, 0.0)
    return pick


class Sizes:
    pass


ORDER = ((1, 1, 1), (0, 1, 1), (1, 0, 1), (0, 0, 1), (1, 1, 0), (0, 1, 0), (1, 0, 0), (0, 0, 0))

EARLY = (
    (2, (
        ("yq", 1, 1),
    )),
)
LATE = (
    ("xp", 1, 1, 1), ("lo", 0), ("ln2",), ("tok",), ("f", 0), ("yq", 0, 1), ("xp", 1, 0, 1), ("xp", 0, 0, 1),
    ("f", 1), ("af", 6), ("v", 0), ("v", 1), ("e", 0), ("xp", 0, 1, 1), ("ig", 0), ("ar", 1, 1), ("yp", 1, 1),
    ("aq", 1), ("v", 2), ("yp", 0, 1), ("e", 1), ("af", 7), ("ar", 0, 1), ("ap", 1), ("lo", 1), ("yq", 1, 0),
    ("ar", 1, 0), ("xp", 1, 0, 0), ("xq", 1), ("v", 3), ("ar", 0, 0), ("yq", 0, 0), ("xp", 1, 1, 0), ("xp", 0, 1, 0),
    ("yr", 1), ("yr", 0), ("e", 2), ("aq", 0), ("xr", 1), ("v", 4), ("xp", 0, 0, 0), ("yp", 1, 0), ("ig", 1),
    ("yp", 0, 0), ("e", 3), ("v", 5), ("ap", 0), ("xr", 0), ("e", 4), ("xq", 0),
)

def layer_kernel(
    z,
    cnt, x_hbm, ct_hbm, ex, co, uplift, offset, scal, cent, resc, rece, lowr, rais, w1_hbm, w2_hbm,
    ro, ro2, fin, ecf, vec,
    x, w1, w2, xs, sb, rb, et, cc, nb16, tp, ta, mixed, nr, ol, yacc, gacc, mgrad, bias, ext, act_s, slope_s, low_s, sums,
    gs, r1, rxp, ryp, rap, rbp, ryq, raq, rxq, rbq, rar, ryr, rxr, rbr,
    vv, vr, ec, ecr, es, er, tg16,
    lsem, a_s, a_r, w_s, w_r, c_s, c_r, xp_s, xp_r, yp_s, yp_r, ap_s, ap_r, bp_s, bp_r,
    yq_s, yq_r, aq_s, aq_r, xq_s, xq_r, bq_s, bq_r, ar_s, ar_r, yr_s, yr_r, xr_s, xr_r, br_s, br_r,
    o_s, o_r, v_s, v_r, e_s, e_r,
):
    D, PT, PP, R, HB, HC, T, NDP = z.D, z.PT, z.PP, z.R, z.HB, z.HC, z.T, z.NDP
    DSL, DS = z.DSL, z.DSL * T
    PL = PP * T
    half_r = R // 2
    dp = lax.axis_index("dp")
    te = lax.axis_index("tensor")
    di = lax.rem(dp, NDP)
    mc = lax.rem(te, 2)
    mx = te // 2
    my = lax.rem(di, 2)
    mz = di // 2

    def tpeer(o):
        if o == 1:
            return te + 1 - 2 * mc
        if o == 2:
            return lax.rem(te + 2, 4)
        return 3 - te

    core_dev = (dp, tpeer(1))
    x_dev = (dp, tpeer(2))
    y_dev = (dp + 1 - 2 * my, te)

    a_dev = (dp + 2 - 4 * lax.rem(mz, 2), te)
    b_dev = (dp - di + lax.rem(di + 4, NDP), te)
    ma, mb = lax.rem(mz, 2), mz // 2

    def rc(src, dst, ss, rs, dev):
        return pltpu.make_async_remote_copy(
            src_ref=src, dst_ref=dst, send_sem=ss, recv_sem=rs, device_id=dev, device_id_type=MESH
        )

    sent = []

    def send(copy):
        copy.start()
        sent.append(copy)

    lc_ct = pltpu.make_async_copy(ct_hbm, x, lsem.at[0])
    lc_w1 = pltpu.make_async_copy(w1_hbm, w1, lsem.at[1])
    lc_w2 = pltpu.make_async_copy(w2_hbm, w2, lsem.at[2])
    lc_x = pltpu.make_async_copy(x_hbm, x, lsem.at[5])
    lc_x.start()

    peers = [(dp, tpeer(o)) for o in (1, 2, 3)] + [y_dev, a_dev, b_dev]
    bar = pltpu.get_barrier_semaphore()
    for dev in peers:
        pl.semaphore_signal(bar, inc=1, device_id=dev, device_id_type=MESH)

    row8 = lax.broadcasted_iota(jnp.int32, (8, LANES), 0)
    PM = PT - PT % 8
    IMG = (slice(0, PM), slice(PP, PP + PM))
    IN = (pl.ds(0, PP), pl.ds(PP, PM))
    OUT = (pl.ds(0, PM), pl.ds(PM, PP))

    def spread(src, k):
        for c in range(D // LANES):
            lanes = slice(c * LANES, (c + 1) * LANES)
            base = c * PT * 8
            xs[base : base + PT * 8, :] = src[:, :, lanes].astype(F32).reshape(PT * 8, LANES)
            tail = xs[base + PM * 8 : base + PT * 8, :]
            for j in range(T):
                for b in range(2):
                    sb[k, j, IMG[b], lanes] = xs[pl.ds(base + 2 * j + b, PM, stride=8), :].astype(BF16)
                two = tail if j == 0 else pltpu.roll(tail, 8 - 2 * j, 0)
                sb[k, j, PM:PP, lanes] = jnp.where(row8 < 2, two, 0.0).astype(BF16)

    def a2a(k, o, b):
        j = tpeer(o)
        return rc(sb.at[k, j, IN[b]], rb.at[k, te, IN[b]], a_s.at[k, o - 1, b], a_r.at[k, o - 1, b], (dp, j))

    def a2a_in(k, o, b):
        j = tpeer(o)
        return rc(sb.at[k, j, IN[b]], rb.at[k, j, IN[b]], a_s.at[k, o - 1, b], a_r.at[k, o - 1, b], (dp, j))

    lc_x.wait()
    spread(x, 0)
    lc_ct.start()
    pl.semaphore_wait(bar, len(peers))
    for o in (2, 3, 1):
        a2a(0, o, 0).start()

    pick = pick_matrix(T, PT, PP)
    pick16 = pick.astype(BF16)
    col1 = lax.broadcasted_iota(jnp.int32, (1, PL), 1)
    pad_one = jnp.where(col1 == PT, 1.0, 0.0)
    uplift_col = dot_exact(uplift[...].astype(F32).reshape(1, DSL), pad_one, 0, 0)
    et[te, 0] = (dot(ex[...], pick16, 1, 0) + uplift_col).astype(BF16)
    et[te, 1] = dot(co[...], pick16, 1, 0).astype(BF16)
    off_line = offset[...].astype(F32).reshape(1, PT)
    own_cols = (lax.broadcasted_iota(jnp.int32, (PT, PL), 1) - PP * te) == lax.broadcasted_iota(
        jnp.int32, (PT, PL), 0
    )
    off_row = dot(off_line.astype(BF16), jnp.where(own_cols, 1.0, 0.0).astype(BF16), 1, 0)
    cc[te] = jnp.broadcast_to(off_row, (8, PL))

    tx, t3 = tpeer(2), tpeer(3)

    def wcopy(k, ref, dev):
        return rc(ref, ref, w_s.at[k], w_r.at[k], dev)

    send(wcopy(0, et.at[te, my], x_dev))
    send(wcopy(1, cc.at[te], x_dev))
    for o in (2, 3, 1):
        a2a(0, o, 1).start()
    send(wcopy(2, et.at[te], core_dev))
    send(wcopy(3, cc.at[te], core_dev))
    rb[0, te] = sb[0, te]

    lc_ct.wait()
    lc_w1.start()
    lc_w2.start()
    spread(x, 1)
    for b in range(2):
        for o in (2, 3, 1):
            a2a(1, o, b).start()
    rb[1, te] = sb[1, te]

    wcopy(0, et.at[tx, my], x_dev).wait_recv()
    send(wcopy(4, et.at[tx, my], y_dev))
    wcopy(1, cc.at[tx], x_dev).wait_recv()
    send(wcopy(5, et.at[tx, my], core_dev))
    send(wcopy(6, cc.at[tx], core_dev))
    bias_line = rais[...].astype(F32).reshape(1, HB * NDP)
    for m in range(NDP // 2):
        bias[m : m + 1, :] = bias_line[:, 2 * m * HB : 2 * (m + 1) * HB]
    scaling, centering = scal[...].astype(F32).reshape(1, D), cent[...].astype(F32).reshape(1, D)
    rescaling, recentering = resc[...].astype(F32).reshape(1, D), rece[...].astype(F32).reshape(1, D)
    lowering = lowr[...].astype(F32).reshape(1, D)
    wcopy(4, et.at[tx, 1 - my], y_dev).wait_recv()
    send(wcopy(7, et.at[tx, 1 - my], core_dev))
    tc = tpeer(1)
    for k, ref in ((2, et.at[tc]), (3, cc.at[tc]), (5, et.at[t3, my]), (6, cc.at[t3]), (7, et.at[t3, 1 - my])):
        wcopy(k, ref, core_dev).wait_recv()

    e_t = et[:, 0].reshape(DS, PL)
    c_t = et[:, 1].reshape(DS, PL)
    zero_pad = lax.broadcasted_iota(jnp.int32, (DS, PL), 1) == PT
    e_clean = jnp.where(zero_pad, 0.0, e_t.astype(F32)).astype(BF16)
    off_full = (cc[0] + cc[1]) + (cc[2] + cc[3])
    first8 = lax.broadcasted_iota(jnp.int32, (8, PL), 0) == 0
    off_row8 = jnp.where(first8, off_full, 0.0).astype(BF16)
    ones_row = lax.broadcasted_iota(jnp.int32, (half_r, 1), 0) == PT
    row8d = lax.broadcasted_iota(jnp.int32, (8, D), 0)
    ones8 = jnp.where(row8d == 0, 1.0, 0.0).astype(BF16)

    def image_rows(k, b):
        pieces = []
        for t in range(T):
            tail = rb[k, t, PM:PP, :].astype(F32)
            tail = pltpu.roll(tail, 7, 0) if b else tail
            pieces += [rb[k, t, IMG[b], :].astype(F32), jnp.where(row8d == 0, tail, 0.0)]
        return jnp.concatenate(pieces, axis=0)

    for b in range(2):
        for o in (1, 2, 3):
            a2a_in(0, o, b).wait_recv()
        sl = slice(b * half_r, (b + 1) * half_r)
        xb = image_rows(0, b)
        xhat, _ = norm_stats(xb)
        n = jnp.where(ones_row, 1.0, xhat * scaling + centering).astype(BF16)
        nb16[sl, :] = n
        pre = dot(e_t, n, 1, 0)
        tp[b] = pre
        act, _ = gelu_parts(pre)
        ta[b, 0:DS, :] = act.astype(BF16)
        ta[b, DS : DS + 8, :] = ones8
        mx_b = xb + dot(c_t, ta[b, 0:DS, :], 0, 0) + dot(off_row8, ones8, 0, 0)
        mixed[sl, :] = mx_b
        xh2, _ = norm_stats(mx_b)
        nr[sl, :] = (xh2 * rescaling + recentering).astype(BF16)

    def flip(m, bit):
        return m + bit - 2 * m * bit

    def pair(k):
        m = flip(mb, 1 - k // 2) * 2 + flip(ma, 1 - k % 2)
        return m, pl.ds(pl.multiple_of(m * 2 * HB, 2 * HB), 2 * HB)

    def ahead(k):
        m, cols = pair(k)
        act, slope = gelu_parts(dot(nr[...], w1[:, cols], 1, 0) + bias[pl.ds(m, 1), :])
        act_s[...] = act.astype(BF16)
        slope_s[...] = slope

    yacc[...] = jnp.zeros(yacc.shape, F32)
    gacc[...] = jnp.zeros(gacc.shape, F32)
    vv[0] = jnp.zeros(vv.shape[1:], F32)
    lc_w1.wait()
    lc_w2.wait()
    ahead(0)
    low_sum = jnp.zeros((1, D), F32)
    for b in range(2):
        for o in (1, 2, 3):
            a2a_in(1, o, b).wait_recv()
        sl = slice(b * half_r, (b + 1) * half_r)
        keep = jnp.where(2 * te + b < cnt[0], 1.0, 0.0)
        og = image_rows(1, b) * keep
        ol[sl, :] = og.astype(BF16)
        low_sum = low_sum + jnp.sum(og, axis=0, keepdims=True)
    vv[0, 4:5, 0:D] = low_sum

    PR, QR, RR = pl.ds(0, z.P), pl.ds(z.P, z.Q), pl.ds(z.P + z.Q, HC - z.P - z.Q)
    pos = {o: i for i, o in enumerate(ORDER)}

    def add_into(dst, src):
        dst[...] = (dst[...].astype(F32) + src[...].astype(F32)).astype(BF16)

    def piece(o, rows, xx):
        if xx is None:
            return gs.at[pos[o], mc, :, :, rows]
        return gs.at[pos[o], mc, xx, :, rows]

    def core_copy(i):
        return rc(gs.at[i, 1 - mc], r1.at[i], c_s.at[i], c_r.at[i], core_dev)

    def xp_copy(i):
        return rc(gs.at[i, mc, 1 - mx, :, PR], rxp.at[i], xp_s.at[i], xp_r.at[i], x_dev)

    def yq_copy(i):
        k = i // 2
        return rc(gs.at[i, mc, :, :, QR], ryq.at[k], yq_s.at[k], yq_r.at[k], y_dev)

    def ar_copy(i):
        k = i // 4 * 2 + i % 2
        return rc(gs.at[i, mc, :, :, RR], rar.at[k], ar_s.at[k], ar_r.at[k], a_dev)

    def yp_copy(da, db):
        k = 2 * da + db
        return rc(piece((1, da, db), PR, mx), ryp.at[k], yp_s.at[k], yp_r.at[k], y_dev)

    def ap_copy(db):
        return rc(piece((0, 1, db), PR, mx), rap.at[db], ap_s.at[db], ap_r.at[db], a_dev)

    def aq_copy(db):
        return rc(piece((0, 1, db), QR, None), raq.at[db], aq_s.at[db], aq_r.at[db], a_dev)

    def xq_copy(db):
        return rc(piece((0, 0, db), QR, 1 - mx), rxq.at[db], xq_s.at[db], xq_r.at[db], x_dev)

    def yr_copy(db):
        return rc(piece((1, 0, db), RR, None), ryr.at[db], yr_s.at[db], yr_r.at[db], y_dev)

    def xr_copy(db):
        return rc(piece((0, 0, db), RR, 1 - mx), rxr.at[db], xr_s.at[db], xr_r.at[db], x_dev)

    bp_copy = rc(piece((0, 0, 1), PR, mx), rbp, bp_s, bp_r, b_dev)
    bq_copy = rc(piece((0, 0, 1), QR, mx), rbq, bq_s, bq_r, b_dev)
    br_copy = rc(piece((0, 0, 1), RR, mx), rbr, br_s, br_r, b_dev)

    def xp(dy, da, db):
        o = (dy, da, db)
        return xp_copy(pos[o]), o, PR, rxp.at[pos[o]], False, [yp_copy(da, db)] if dy else []

    def yp(da, db):
        return yp_copy(da, db), (0, da, db), PR, ryp.at[2 * da + db], False, [ap_copy(db)] if da else []

    def ap(db):
        return ap_copy(db), (0, 0, db), PR, rap.at[db], False, [bp_copy] if db else []

    def yq(da, db):
        i = pos[1, da, db]
        return yq_copy(i), (0, da, db), QR, ryq.at[i // 2], True, [aq_copy(db)] if da else []

    def aq(db):
        return aq_copy(db), (0, 0, db), QR, raq.at[db], True, [xq_copy(db)]

    def xq(db):
        return xq_copy(db), (0, 0, db), QR, rxq.at[db], False, [bq_copy] if db else []

    def ar(dy, db):
        i = pos[dy, 1, db]
        return ar_copy(i), (dy, 0, db), RR, rar.at[i // 4 * 2 + i % 2], True, [yr_copy(db)] if dy else []

    def yr(db):
        return yr_copy(db), (0, 0, db), RR, ryr.at[db], True, [xr_copy(db)]

    def xr(db):
        return xr_copy(db), (0, 0, db), RR, rxr.at[db], False, [br_copy] if db else []

    steps = dict(xp=xp, yp=yp, ap=ap, yq=yq, aq=aq, xq=xq, ar=ar, yr=yr, xr=xr)

    def take(name, *bits):
        arrival, o, rows, src, both, on = steps[name](*bits)
        arrival.wait_recv()
        for g in range(2):
            if both:
                for xx in range(2):
                    add_into(gs.at[pos[o], mc, xx, g, rows], src.at[xx, g])
            else:
                add_into(gs.at[pos[o], mc, mx, g, rows], src.at[g])
        for c in on:
            c.start()
        return on

    def af(i):
        core_copy(i).wait_recv()
        for xx in range(2):
            for g in range(2):
                add_into(gs.at[i, mc, xx, g], r1.at[i, xx, g])

    def first_hops(i):
        dy, da, _ = ORDER[i]
        if dy:
            yq_copy(i).start()
        if da:
            ar_copy(i).start()
        xp_copy(i).start()

    for k in range(NDP // 2):
        m, cols = pair(k)
        low16 = (slope_s[...] * dot(ol[...], w2[cols, :], 1, 1)).astype(BF16)
        low_s[...] = low16
        line = jnp.sum(low16.astype(F32), axis=0, keepdims=True)
        for y in range(2):
            vv[0, pl.ds(2 * m + y, 1), D : D + HB] = line[:, y * HB : (y + 1) * HB]
        if k > 0:
            for i in (2 * k - 2, 2 * k - 1):
                af(i)
                first_hops(i)
        gn = dot(act_s[...], ol[...], 0, 0)
        gb = dot(low_s[...], nr[...], 0, 0)
        for y, h in ((0, 1 - my), (1, my)):
            for t in range(T):
                rows = slice(y * HB + t * HC, y * HB + (t + 1) * HC)
                gs[2 * k + h, t % 2, t // 2, 0] = gn[rows, :].astype(BF16)
                gs[2 * k + h, t % 2, t // 2, 1] = gb[rows, :].astype(BF16)
        for h in range(2):
            core_copy(2 * k + h).start()
        yacc[...] += dot(act_s[...], w2[cols, :], 1, 0)
        gacc[...] += dot(low_s[...], w1[:, cols], 1, 1)
        if k + 1 < NDP // 2:
            ahead(k + 1)
        for at, ops in EARLY:
            if at == k:
                for op in ops:
                    take(*op)

    sent.extend([core_copy(i) for i in range(NDP)] + [xp_copy(i) for i in range(NDP)])
    sent.extend([yq_copy(i) for i, o in enumerate(ORDER) if o[0]] + [ar_copy(i) for i, o in enumerate(ORDER) if o[1]])
    for _, ops in EARLY:
        for op in ops:
            sent.extend(steps[op[0]](*op[1:])[-1])

    so, so2 = sb.at[0], sb.at[1]
    for k in range(2):
        for o in (1, 2, 3):
            for b in range(2):
                a2a(k, o, b).wait_send()

    def ocopy(k, o, b):
        src, dst = (so, ro) if k == 0 else (so2, ro2)
        j = tpeer(o)
        return rc(src.at[j, OUT[b]], dst.at[te, OUT[b]], o_s.at[k, o - 1, b], o_r.at[k, o - 1, b], (dp, j))

    def ocopy_in(k, o, b):
        src, dst = (so, ro) if k == 0 else (so2, ro2)
        j = tpeer(o)
        return rc(src.at[j, OUT[b]], dst.at[j, OUT[b]], o_s.at[k, o - 1, b], o_r.at[k, o - 1, b], (dp, j))

    lc_o = [pltpu.make_async_copy(s.at[te], r.at[te], lsem.at[3 + k]) for k, (s, r) in enumerate(((so, ro), (so2, ro2)))]

    def pack(k, b, t, rows):
        dst = so if k == 0 else so2
        dst[t, IMG[b], :] = rows[0:PM, :].astype(BF16)
        tail = jnp.where(row8d == 0, rows[PM:PP, :], 0.0)
        if b == 0:
            ext[k, t] = tail
        else:
            dst[t, PM:PP, :] = (ext[k, t] + pltpu.roll(tail, 1, 0)).astype(BF16)

    def go(k, b):
        for o in (2, 3, 1):
            send(ocopy(k, o, b))
        if b == 1:
            lc_o[k].start()

    def part(b):
        return slice(b * half_r, (b + 1) * half_r)

    def lo(b):
        keep = jnp.where(2 * te + b < cnt[0], 1.0, 0.0)
        for t in range(T):
            sl = slice(b * half_r + t * PP, b * half_r + (t + 1) * PP)
            pack(0, b, t, (mixed[sl, :] + yacc[sl, :] + lowering) * keep)
        go(0, b)

    def ln2():
        resc_sum = jnp.zeros((1, D), F32)
        rece_sum = jnp.zeros((1, D), F32)
        for b in range(2):
            xh2, rs2 = norm_stats(mixed[part(b), :])
            gr = gacc[part(b), :]
            resc_sum = resc_sum + jnp.sum(gr * xh2, axis=0, keepdims=True)
            rece_sum = rece_sum + jnp.sum(gr, axis=0, keepdims=True)
            mgrad[part(b), :] = ol[part(b), :].astype(F32) + norm_back(gr, xh2, rs2, rescaling)
        vv[0, 2:3, 0:D] = resc_sum
        vv[0, 3:4, 0:D] = rece_sum

    hops = (x_dev, b_dev, a_dev, y_dev)
    e_core = rc(ec.at[1 - mc], ecr, e_s.at[0], e_r.at[0], core_dev)

    def v_copy(s):
        return rc(vv.at[s], vr.at[s], v_s.at[s], v_r.at[s], ((core_dev,) + hops)[s])

    def e_copy(s):
        return rc(es.at[s], er.at[s], e_s.at[s + 1], e_r.at[s + 1], hops[s])

    def tok():
        eg_sum = jnp.zeros((DS, PL), F32)
        cg_sum = jnp.zeros((DS + 8, PL), F32)
        for b in range(2):
            ml = mgrad[part(b), :].astype(BF16)
            _, slope = gelu_parts(tp[b])
            tg = (slope * dot(c_t, ml, 1, 0)).astype(BF16)
            tg16[b] = tg
            cg_sum = cg_sum + dot(ta[b], ml, 1, 1)
            eg_sum = eg_sum + dot(tg, nb16[part(b), :], 1, 1)
        vv[0, 5:6, 0:PL] = cg_sum[DS : DS + 1, :]
        for t in range(T):
            ec[t % 2, t // 2, 0] = eg_sum[t * DSL : (t + 1) * DSL, :]
            ec[t % 2, t // 2, 1] = cg_sum[t * DSL : (t + 1) * DSL, :]
        send(e_core)

    def f(b):
        nback = dot(e_clean, tg16[b], 0, 0)
        xhat, rs1 = norm_stats(image_rows(0, b))
        grad = mgrad[part(b), :] + norm_back(nback, xhat, rs1, scaling)
        for t in range(T):
            pack(1, b, t, grad[t * PP : (t + 1) * PP, :])
        sums[2 * b : 2 * b + 1, :] = jnp.sum(nback * xhat, axis=0, keepdims=True)
        sums[2 * b + 1 : 2 * b + 2, :] = jnp.sum(nback, axis=0, keepdims=True)

    def ig(b):
        go(1, b)

    def e(s):
        if s == 0:
            e_core.wait_recv()
            es[0] = (ec[mc, 1 - mx] + ecr[1 - mx]).astype(BF16)
            send(e_copy(0))
            return
        e_copy(s - 1).wait_recv()
        if s == 1:
            tot = ec[mc, mx] + ecr[mx] + er[0].astype(F32)
        else:
            tot = es[s - 1].astype(F32) + er[s - 1].astype(F32)
        if s == 4:
            ecf[...] = tot
        else:
            es[s] = tot.astype(BF16)
            send(e_copy(s))

    def v(s):
        if s == 0:
            for r in range(2):
                vv[0, r : r + 1, 0:D] = sums[r : r + 1, :] + sums[r + 2 : r + 3, :]
        else:
            v_copy(s - 1).wait_recv()
            vv[s] = vv[s - 1] + vr[s - 1]
        if s < 5:
            send(v_copy(s))

    def last_block(i):
        af(i)
        first_hops(i)

    work = dict(af=last_block, ln2=ln2, tok=tok, f=f, lo=lo, ig=ig, e=e, v=v)
    for op in LATE:
        if op[0] in work:
            work[op[0]](*op[1:])
        else:
            sent.extend(take(*op))

    for copy, rows, buf in ((bq_copy, QR, rbq), (br_copy, RR, rbr), (bp_copy, PR, rbp)):
        copy.wait_recv()
        for g in range(2):
            fin[g, rows, :] = gs[NDP - 1, mc, mx, g, rows, :].astype(F32) + buf[g].astype(F32)
    vec[...] = vv[5]
    for k in range(2):
        for o in (1, 2, 3):
            for b in range(2):
                ocopy_in(k, o, b).wait_recv()
        lc_o[k].wait()

    for c in sent:
        c.wait_send()


def finish_kernel(
    z, ro_h, ro2_h, fin_h, ecf_h, vec_h, lo, ig, eg, up, cg, off, v0, v1, v2, v3, bg, rg, ng, v4,
    xs, ro, ro2, ecf, vec, sem,
):
    D, PT, PP, HB, HC, T, NDP, DSL = z.D, z.PT, z.PP, z.HB, z.HC, z.T, z.NDP, z.DSL
    PM = PT - PT % 8
    te = lax.axis_index("tensor")
    di = lax.rem(lax.axis_index("dp"), NDP)
    pairs = ((ro_h, ro), (ro2_h, ro2), (ecf_h, ecf), (vec_h, vec), (fin_h.at[0], ng), (fin_h.at[1], bg))
    loads = [pltpu.make_async_copy(src, dst, sem.at[k]) for k, (src, dst) in enumerate(pairs)]
    for c in loads:
        c.start()
    for k, (src, dst) in enumerate(((ro, lo), (ro2, ig))):
        loads[k].wait()
        for c in range(D // LANES):
            lanes = slice(c * LANES, (c + 1) * LANES)
            base = c * PT * 8
            for j in range(T):
                for b, at in ((0, 0), (1, PP)):
                    xs[pl.ds(base + 2 * j + b, PM, stride=8), :] = src[j, at : at + PM, lanes].astype(F32)
                last = base + PM * 8 + 2 * j
                xs[last : last + 2, :] = src[j, PM:PP, lanes].astype(F32)[0:2, :]
            dst[:, :, lanes] = xs[base : base + PT * 8, :].reshape(PT, 8, LANES).astype(BF16)
    for c in loads[2:]:
        c.wait()
    pick = pick_matrix(T, PT, PP)
    eg[...] = dot_exact(ecf[0], pick, 1, 1)
    cg[...] = dot_exact(ecf[1], pick, 1, 1)
    row8 = lax.broadcasted_iota(jnp.int32, (8, PP * T), 1)
    up[...] = dot_exact(jnp.where(row8 == PT, 1.0, 0.0), ecf[0], 1, 1)[0:1, :].reshape(DSL)
    for ref, r in ((v0, 0), (v1, 1), (v2, 2), (v3, 3), (v4, 4)):
        ref[...] = vec[r : r + 1, 0:D].reshape(D)
    off_row = vec[5:6, :]
    rg_row = vec[pl.ds(di, 1), D:]
    off_own = jnp.zeros((1, PT), F32)
    rg_own = jnp.zeros((1, HC), F32)
    for t in range(T):
        off_own = off_own + jnp.where(te == t, off_row[:, t * PP : t * PP + PT], 0.0)
        rg_own = rg_own + jnp.where(te == t, rg_row[:, t * HC : (t + 1) * HC], 0.0)
    off[...] = off_own.reshape(PT)
    rg[...] = rg_own.reshape(HC)


def local(
    layer_input, image_counts, expand, uplift, contract, offset, scaling, centering,
    rescaling, recentering, broaden, raising, narrow, lowering, cotangent, *, mesh,
):
    z = Sizes()
    z.PT, images, z.D = layer_input.shape
    z.T, z.NDP = mesh.shape["tensor"], 8
    outer = mesh.shape["dp"] // z.NDP
    z.PP = -(-(z.PT + 1) // 8) * 8
    z.R = 2 * z.T * z.PP
    hidden = broaden.shape[1]
    if outer > 1:
        split = (outer, z.NDP, z.T, hidden // (outer * z.NDP * z.T))
        broaden = broaden.reshape(-1, *split).transpose(0, 2, 3, 1, 4).reshape(-1, hidden)
        raising = raising.reshape(split).transpose(1, 2, 0, 3).reshape(hidden)
        narrow = narrow.reshape(*split, -1).transpose(1, 2, 0, 3, 4).reshape(hidden, -1)
    z.HB = hidden // z.NDP
    z.HC = z.HB // z.T
    z.DSL = expand.shape[1]
    D, T, NDP, PP, PT, R, HB, HC, DSL = z.D, z.T, z.NDP, z.PP, z.PT, z.R, z.HB, z.HC, z.DSL
    DS, PL, PK = DSL * T, PP * T, PP + PT - PT % 8

    vm = pl.BlockSpec(memory_space=pltpu.VMEM)
    anys = pl.BlockSpec(memory_space=pl.ANY)
    dma = pltpu.SemaphoreType.DMA
    V = pltpu.VMEM
    S = jax.ShapeDtypeStruct
    z.P, z.Q = HC * 4 // 12, HC * 4 // 12
    P_, Q_, R_ = z.P, z.Q, HC - z.P - z.Q
    sems = []
    for shape in (
        (2, 3, 2), (8,), (NDP,), (NDP,), (4,), (2,), (), (4,), (2,), (2,), (), (4,), (2,), (2,), (),
        (2, 3, 2), (5,), (5,),
    ):
        sems += [dma(shape), dma(shape)]
    scratch = [
        V((PT, 8, D), BF16), V(broaden.shape, BF16), V(narrow.shape, BF16), V((D // LANES * PT * 8, LANES), F32),
        V((2, T, PK, D), BF16), V((2, T, PK, D), BF16), V((T, 2, DSL, PL), BF16), V((T, 8, PL), F32),
        V((R, D), BF16), V((2, DS, D), F32), V((2, DS + 8, D), BF16), V((R, D), F32), V((R, D), BF16), V((R, D), BF16),
        V((R, D), F32), V((R, D), F32), V((R, D), F32), V((NDP // 2, 2 * HB), F32),
        V((2, T, 8, D), F32), V((R, 2 * HB), BF16), V((R, 2 * HB), F32), V((R, 2 * HB), BF16), V((4, D), F32),
        V((NDP, 2, 2, 2, HC, D), BF16), V((NDP, 2, 2, HC, D), BF16),
        V((NDP, 2, P_, D), BF16), V((4, 2, P_, D), BF16), V((2, 2, P_, D), BF16), V((2, P_, D), BF16),
        V((4, 2, 2, Q_, D), BF16), V((2, 2, 2, Q_, D), BF16), V((2, 2, Q_, D), BF16), V((2, Q_, D), BF16),
        V((4, 2, 2, R_, D), BF16), V((2, 2, 2, R_, D), BF16), V((2, 2, R_, D), BF16), V((2, R_, D), BF16),
        V((6, 8, D + HB), F32), V((5, 8, D + HB), F32), V((2, 2, 2, DSL, PL), F32), V((2, 2, DSL, PL), F32),
        V((4, 2, DSL, PL), BF16), V((4, 2, DSL, PL), BF16), V((2, DS, D), BF16),
        dma((6,)),
    ] + sems
    mid = pl.pallas_call(
        functools.partial(layer_kernel, z),
        out_shape=(
            S((T, PK, D), BF16), S((T, PK, D), BF16), S((2, HC, D), F32), S((2, DSL, PL), F32), S((8, D + HB), F32),
        ),
        in_specs=[pl.BlockSpec(memory_space=pltpu.SMEM), anys, anys] + [vm] * 10 + [anys, anys],
        out_specs=(anys, anys, vm, vm, vm),
        scratch_shapes=scratch,
        compiler_params=pltpu.CompilerParams(
            collective_id=0, has_side_effects=True, vmem_limit_bytes=62 * 1024 * 1024
        ),
    )(
        image_counts, layer_input, cotangent, expand.T, contract, uplift, offset, scaling, centering,
        rescaling, recentering, lowering, raising, broaden, narrow,
    )
    res = pl.pallas_call(
        functools.partial(finish_kernel, z),
        out_shape=(
            S((PT, images, D), BF16), S((PT, images, D), BF16), S((DSL, PT * T), F32), S((DSL,), F32),
            S((DSL, PT * T), F32), S((PT,), F32), S((D,), F32), S((D,), F32), S((D,), F32), S((D,), F32),
            S((HC, D), F32), S((HC,), F32), S((HC, D), F32), S((D,), F32),
        ),
        in_specs=[anys] * 5,
        out_specs=(vm,) * 14,
        scratch_shapes=[
            V((D // LANES * PT * 8, LANES), F32), V((T, PK, D), BF16), V((T, PK, D), BF16), V((2, DSL, PL), F32),
            V((8, D + HB), F32), dma((6,)),
        ],
        compiler_params=pltpu.CompilerParams(vmem_limit_bytes=60 * 1024 * 1024),
    )(*mid)
    lo, ig, eg, up, cg, off, v0, v1, v2, v3, bg, rg, ng, v4 = res
    if outer > 1:
        same = [[o * NDP + i for o in range(outer)] for i in range(NDP)]
        eg, up, cg, off, v0, v1, v2, v3, v4 = lax.psum(
            (eg, up, cg, off, v0, v1, v2, v3, v4), "dp", axis_index_groups=same
        )
        bg, ng, rg = (
            lax.psum_scatter(v, "dp", scatter_dimension=0, axis_index_groups=same, tiled=True) for v in (bg, ng, rg)
        )
    return lo, ig, eg.T, up, cg, off, v0, v1, v2, v3, bg.T, rg, ng, v4


def solution(mesh):
    rows = P("tensor", "dp", None)
    both = ("dp", "tensor")
    in_specs = (
        rows, P("dp"), P(None, "tensor"), P("tensor"), P("tensor", None), P("tensor"),
        P(), P(), P(), P(), P(), P(), P(), P(), rows,
    )
    out_specs = (
        rows, rows, P(None, "tensor"), P("tensor"), P("tensor", None), P("tensor"),
        P(), P(), P(), P(), P(None, both), P(both), P(both, None), P(),
    )
    return jax.shard_map(
        functools.partial(local, mesh=mesh), mesh=mesh, in_specs=in_specs, out_specs=out_specs, check_vma=False
    )
```
